128 devices in a mesh: pool: 2 (over z_hi), dev: 64 (over x, z_lo, y, core).
Axes of the slice: x: 4, y: 4, z: 4 (z_hi: 2, z_lo: 2; z = z_hi * 2 + z_lo), core: 2. Of those that a mesh axis runs over, the one named last changes fastest.
Arguments:
- queries: bfloat16 [2048, 4096], P(('pool', 'dev')), may hold values from -6 to 6
- new_kv: bfloat16 [2048, 512], P(('pool', 'dev')), may hold values from -6 to 6
- kv_pages: bfloat16 [16384, 16, 512], P(('pool', 'dev')), may hold values from -6 to 6
- page_table: int32 [2048, 16], P(('pool', 'dev')), may hold values from 0 to 143, as said below
- lengths: int32 [2048], P(('pool', 'dev')), may hold values from 1 to 256, as said below
- shed_slots: int32 [2048], P(('pool', 'dev')), may hold values from 0 to 127, as said below
- residual: bfloat16 [2048, 4096], P(('pool', 'dev')), may hold values from -6 to 6
- norm_gain: float32 [4096], replicated, may hold values from 0.1 to 1.9
- expert_ids: int32 [2048, 8], P(('pool', 'dev')), may hold values from 0 to 127, all different within a row; in each aligned block of 16 rows (0 to 15, 16 to 31, ...) at most 2 rows name the same one
- gate_weights: float32 [2048, 8], P(('pool', 'dev')), may hold values from 0.05 to 0.6
- w_gate_up: bfloat16 [128, 4096, 1536], P(('pool', 'dev')), may hold values from -0.09375 to 0.09375
- w_down: bfloat16 [128, 768, 4096], P(('pool', 'dev')), may hold values from -0.21875 to 0.21875
Outputs:
- attended: bfloat16 [2048, 4096], P(('pool', 'dev'))
- layer_out: bfloat16 [2048, 4096], P(('pool', 'dev'))
The draws below stay inside these ranges and needn't reach their ends.
Inputs may be any that keep to these rules, and one draw needn't show every extreme that they name: `page_table`: entry p of request r is used for p < ceil(lengths[r] / 16) and is 0 otherwise. The used entries of one device's requests are distinct. Of two partners exactly one sheds: its used entries take every value from 0 to 143; the other's stay below 128. `lengths`: A device that sheds has a request of 256 tokens. `shed_slots`: for a device that sheds: distinct pages of the partner's block that no request of the partner uses. For the other device the list is not read. `expert_ids`: among the 16 requests of one device at most 2 name the same expert; the 8 experts of a request differ.
All inputs are finite; a program needn't handle non-finite values.
Results may differ from the reference program's by a relative error of at most 0.014.
Values may be sent and summed in bfloat16 or wider, within the bound.
A program may use at most 128 MiB of HBM per device.

```python
import math
import jax
import jax.numpy as jnp
import numpy as np
from jax import lax

D = 4096
HEAD_DIMENSION = 128
TOPK = 8
HQ = 32
KEY_VALUE_HEADS = 2
MF = 768
PAGE = 16
MAXP = 16
R_DEV = 16
QUERY_GROUP_SIZE = 16
KVW = 512
PAGES_DEV = 128
SHED = 16
REQUESTS = 2048
EXPERTS = 128
CAP = 2


def base_values(key, shape):
    return jnp.clip(jax.random.normal(key, shape, jnp.float32), -6.0, 6.0)


def page_plan(key):
    streams = jax.random.split(jax.random.fold_in(key, 4242), 6)
    device_count = REQUESTS // R_DEV
    half_count = device_count // 2
    pair_count = R_DEV // 2
    low_heavy = jax.random.randint(streams[0], (half_count,), 0, 2)
    heavy_mask = jnp.concatenate([low_heavy, 1 - low_heavy]) == 1
    heavy_pages = jax.random.randint(streams[1], (device_count, pair_count), 2, MAXP + 1)
    heavy_pages = heavy_pages.at[:, 0].set(MAXP)
    heavy_pages = jnp.stack([heavy_pages, MAXP + 2 - heavy_pages], axis=-1).reshape(device_count, R_DEV)
    light_pages = jax.random.randint(streams[2], (device_count, pair_count), 1, MAXP // 2 + 1)
    light_pages = jnp.stack([light_pages, MAXP // 2 + 1 - light_pages], axis=-1).reshape(device_count, R_DEV)
    page_counts = jnp.where(heavy_mask[:, None], heavy_pages, light_pages)
    last_fill = jax.random.randint(streams[3], (device_count, R_DEV), 1, PAGE + 1)
    length_rows = (page_counts - 1) * PAGE + last_fill
    length_rows = length_rows.at[:, 0].set(jnp.where(heavy_mask, MAXP * PAGE, length_rows[:, 0]))
    starts = jnp.cumsum(page_counts, axis=1) - page_counts
    column = jnp.arange(MAXP)
    flat_index = starts[:, :, None] + column[None, None, :]
    in_use = column[None, None, :] < page_counts[:, :, None]
    heavy_total = PAGES_DEV + SHED
    heavy_order = jax.vmap(lambda stream: jax.random.permutation(stream, heavy_total))(jax.random.split(streams[4], device_count))
    light_order = jax.vmap(lambda stream: jax.random.permutation(stream, PAGES_DEV))(jax.random.split(streams[5], device_count))
    light_padded = jnp.concatenate([light_order, jnp.zeros((device_count, SHED), light_order.dtype)], axis=1)
    page_order = jnp.where(heavy_mask[:, None], heavy_order, light_padded)
    clipped = jnp.clip(flat_index, 0, heavy_total - 1).reshape(device_count, R_DEV * MAXP)
    entries = jnp.take_along_axis(page_order, clipped, axis=1).reshape(device_count, R_DEV, MAXP)
    page_rows = jnp.where(in_use, entries, 0)
    light_used = pair_count * (MAXP // 2 + 1)
    spare_slots = light_order[:, light_used:light_used + SHED]
    partner = (jnp.arange(device_count) + half_count) % device_count
    unread_lists = jax.random.randint(jax.random.fold_in(key, 5151), (device_count, SHED), 0, PAGES_DEV)
    unread_lists = unread_lists.at[:, 0].set(0)
    unread_lists = unread_lists.at[:, SHED - 1].set(PAGES_DEV - 1)
    shed_rows = jnp.where(heavy_mask[:, None], spare_slots[partner], unread_lists)
    return (page_rows.reshape(REQUESTS, MAXP).astype(jnp.int32), length_rows.reshape(REQUESTS).astype(jnp.int32), shed_rows.reshape(device_count * SHED).astype(jnp.int32))


def draw_queries(key, part):
    base_rows = base_values(jax.random.fold_in(key, 1), (REQUESTS, HQ * HEAD_DIMENSION))
    return base_rows.astype(jnp.bfloat16)


def draw_new_kv(key, part):
    base_rows = base_values(jax.random.fold_in(key, 2), (REQUESTS, KVW))
    return base_rows.astype(jnp.bfloat16)


def draw_kv_pages(key, part):
    device_count = REQUESTS // R_DEV
    base_rows = base_values(jax.random.fold_in(key, 3), (device_count * PAGES_DEV, PAGE, KVW))
    return base_rows.astype(jnp.bfloat16)


def draw_page_table(key, part):
    return page_plan(key)[0]


def draw_lengths(key, part):
    return page_plan(key)[1]


def draw_shed_slots(key, part):
    return page_plan(key)[2]


def level_of(key, shape, pieces, smallest, top_value):
    factor_of = 1.0
    for dim, blocks in pieces:
        steps = jax.random.uniform(jax.random.fold_in(jax.random.fold_in(key, 6), dim), (blocks,), jnp.float32, smallest / len(pieces), top_value / len(pieces))
        factor_of = factor_of * jnp.repeat(jnp.exp(steps), shape[dim] // blocks).reshape((-1,) + (1,) * (len(shape) - 1 - dim))
    return factor_of


def deal_out(key, own, number, rows, count, top, most, slope):
    ranking = jax.random.permutation(key, count)
    crowded, common = portions_of(count, rows * top, most, slope, True), portions_of(count, rows * top, most, slope, False)
    places = jnp.arange(count)

    def named(sizes, turn):
        used = int((sizes > 0).sum())
        fixed = max(1, used // 4)
        moved = fixed + (places - fixed + turn * (used - fixed)) % max(1, count - fixed)
        return jnp.zeros((count,), jnp.int32).at[ranking[jnp.where(places < fixed, places, moved)]].set(jnp.asarray(sizes, jnp.int32))

    sizes = jnp.where(number % 4 == 0, named(crowded, number // 4), named(common, number - number // 4 - 1))
    mixed = jax.random.permutation(jax.random.fold_in(own, 3), count)
    source_of, taker = mixed[0:count // 2 * 2:2], mixed[1:count // 2 * 2:2]
    room = jnp.minimum(sizes[source_of] - 1, most - sizes[taker]) // 2
    room = jnp.where((source_of == ranking[0]) | (taker == ranking[0]) | (sizes[taker] == 0), 0, jnp.maximum(room, 0))
    moved = jax.random.randint(jax.random.fold_in(own, 4), (count // 2,), 0, 1 << 20) % (room + 1)
    sizes = sizes.at[source_of].add(-moved).at[taker].add(moved)
    members = jnp.searchsorted(jnp.cumsum(sizes), jnp.arange(rows * top), side="right").astype(jnp.int32)
    listing = members.reshape(top, rows).T
    listing = listing[jax.random.permutation(jax.random.fold_in(own, 1), rows)]
    turn = jax.random.randint(jax.random.fold_in(own, 2), (rows, 1), 0, top)
    return jnp.take_along_axis(listing, (jnp.arange(top)[None, :] + turn) % top, axis=1)


def portions_of(count, total, bound, lean, full):
    portions = [(1 << 20) // math.isqrt(grade ** lean) + 1 for grade in range(1, count + 1)]
    largest = bound if full else min(bound, max(-(-total // count), total * portions[0] // sum(portions)))
    least = 1 if total - largest >= count - 1 else 0
    counts, spare = [largest] + [least] * (count - 1), total - largest - least * (count - 1)
    while spare > 0:
        free = [i for i in range(1, count) if counts[i] < largest] or [i for i in range(1, count) if counts[i] < bound]
        mass, left = sum([portions[i] for i in free]), spare
        for i in free:
            addition = min(bound - counts[i], max(1, left * portions[i] // mass), spare)
            counts[i] = counts[i] + addition
            spare = spare - addition
    return np.array(counts)


def noise(stream_key, shape, scale, reach, cuts=(), kind=jnp.bfloat16):
    level = level_of(stream_key, shape, cuts, -0.22, 0.18) if cuts else 1.0
    array = jax.random.normal(stream_key, shape, jnp.float32) * scale * level
    return jnp.minimum(jnp.maximum(array, -reach), reach).astype(kind)


def setup_inputs(seed: int = 0) -> dict:
    seeds = jax.random.split(jax.random.key(seed), 13)
    queries = draw_queries(jax.random.fold_in(seeds[12], 71), 0)
    new_kv = draw_new_kv(jax.random.fold_in(seeds[12], 71), 0)
    kv_pages = draw_kv_pages(jax.random.fold_in(seeds[12], 71), 0)
    page_table = draw_page_table(jax.random.fold_in(seeds[12], 71), 0)
    lengths = draw_lengths(jax.random.fold_in(seeds[12], 71), 0)
    shed_slots = draw_shed_slots(jax.random.fold_in(seeds[12], 71), 0)
    residual = noise(seeds[6], (REQUESTS, D), 1.0, 6.0, ((0, 128),))
    norm_gain = jnp.clip(1.0 + 0.18 * jax.random.normal(seeds[7], (D,), jnp.float32), 0.1, 1.9)
    expert_ids_keys = jax.random.split(jax.random.fold_in(seeds[8], 1), REQUESTS // R_DEV)
    expert_ids_turns = jax.random.permutation(jax.random.fold_in(seeds[8], 3), REQUESTS // R_DEV)
    expert_ids = jax.vmap(lambda own, number: deal_out(jax.random.fold_in(seeds[8], 2), own, number, R_DEV, EXPERTS, TOPK, CAP, 2))(expert_ids_keys, expert_ids_turns).reshape((REQUESTS, TOPK))
    gate_weights = jnp.clip(jnp.exp(math.log(0.6) - 2.4849067 * jax.random.uniform(seeds[9], (REQUESTS, TOPK), jnp.float32) ** level_of(seeds[9], (REQUESTS, TOPK), ((0, 128),), -0.2, 0.2)), 0.05, 0.6)
    w_gate_up = noise(seeds[10], (EXPERTS, D, 2 * MF), D ** -0.5, 0.09375, ((0, 128),))
    w_down = noise(seeds[11], (EXPERTS, MF, D), MF ** -0.5, 0.21875, ((0, 128),))
    return dict(queries=queries, new_kv=new_kv, kv_pages=kv_pages, page_table=page_table, lengths=lengths, shed_slots=shed_slots, residual=residual, norm_gain=norm_gain, expert_ids=expert_ids, gate_weights=gate_weights, w_gate_up=w_gate_up, w_down=w_down)


masked_score = -1e+30
epsilon = 1e-06
highest = lax.Precision.HIGHEST

def attend_rows(source, table_rows, length_rows, query_entries, incoming_rows):
    count_of_rows = table_rows.shape[0]
    key_row_width = incoming_rows.shape[-1] // 2
    collected_rows = jnp.take(source, table_rows, axis=0).reshape(count_of_rows, -1, source.shape[-1])
    key_entries = collected_rows[:, :, :key_row_width].reshape(count_of_rows, -1, KEY_VALUE_HEADS, HEAD_DIMENSION).astype(jnp.float32)
    value_entries = collected_rows[:, :, key_row_width:].reshape(count_of_rows, -1, KEY_VALUE_HEADS, HEAD_DIMENSION).astype(jnp.float32)
    query_head_block = query_entries.reshape(count_of_rows, KEY_VALUE_HEADS, QUERY_GROUP_SIZE, HEAD_DIMENSION).astype(jnp.float32)
    scaling = 1.0 / math.sqrt(HEAD_DIMENSION)
    scores = jnp.einsum('rkgd,rlkd->rkgl', query_head_block, key_entries, precision=highest) * scaling
    positions = jnp.arange(key_entries.shape[1], dtype=jnp.int32)
    allowed = positions[None, :] < length_rows[:, None]
    scores = jnp.where(allowed[:, None, None, :], scores, masked_score)
    incoming_keys = incoming_rows[:, :key_row_width].reshape(count_of_rows, KEY_VALUE_HEADS, HEAD_DIMENSION).astype(jnp.float32)
    incoming_values = incoming_rows[:, key_row_width:].reshape(count_of_rows, KEY_VALUE_HEADS, HEAD_DIMENSION).astype(jnp.float32)
    fresh_score = jnp.einsum('rkgd,rkd->rkg', query_head_block, incoming_keys, precision=highest) * scaling
    largest = jnp.maximum(lax.optimization_barrier(jnp.max(scores, axis=-1)), fresh_score)
    weights = jnp.exp(scores - largest[..., None])
    fresh_weight = jnp.exp(fresh_score - largest)
    denominator = lax.optimization_barrier(jnp.sum(weights, axis=-1)) + fresh_weight
    weights_low = lax.optimization_barrier(weights.astype(jnp.bfloat16)).astype(jnp.float32)
    fresh_low = lax.optimization_barrier(fresh_weight.astype(jnp.bfloat16)).astype(jnp.float32)
    summed = jnp.einsum('rkgl,rlkd->rkgd', weights_low, value_entries, precision=highest)
    summed = summed + fresh_low[..., None] * incoming_values[:, :, None, :]
    return (summed / denominator[..., None]).reshape(count_of_rows, -1).astype(jnp.bfloat16)

def expert_rows(tokens, gate_up, down_proj):
    hidden_dim = down_proj.shape[0]
    product = jnp.dot(tokens, gate_up, preferred_element_type=jnp.float32)
    hidden = (jax.nn.silu(product[:, :hidden_dim]) * product[:, hidden_dim:]).astype(jnp.bfloat16)
    return jnp.dot(hidden, down_proj, preferred_element_type=jnp.float32).astype(jnp.bfloat16)

def reference(queries, new_kv, kv_pages, page_table, lengths, shed_slots, residual, norm_gain, expert_ids, gate_weights, w_gate_up, w_down):
    device_count = REQUESTS // R_DEV

    def per_device(device_index):
        row_start = (device_index * R_DEV).astype(jnp.int32)
        partner = ((device_index + device_count // 2) % device_count).astype(jnp.int32)
        own_pages = lax.dynamic_slice_in_dim(kv_pages, (device_index * PAGES_DEV).astype(jnp.int32), PAGES_DEV, 0)
        other_pages = lax.dynamic_slice_in_dim(kv_pages, (partner * PAGES_DEV).astype(jnp.int32), PAGES_DEV, 0)
        hosted = lax.dynamic_slice_in_dim(shed_slots, (device_index * SHED).astype(jnp.int32), SHED, 0)
        combined = jnp.concatenate([own_pages, jnp.take(other_pages, hosted, axis=0)], axis=0)
        table_rows = lax.dynamic_slice_in_dim(page_table, row_start, R_DEV, 0)
        length_rows = lax.dynamic_slice_in_dim(lengths, row_start, R_DEV, 0)
        query_entries = lax.dynamic_slice_in_dim(queries, row_start, R_DEV, 0)
        incoming_rows = lax.dynamic_slice_in_dim(new_kv, row_start, R_DEV, 0)
        return attend_rows(combined, table_rows, length_rows, query_entries, incoming_rows)
    attended = lax.map(per_device, jnp.arange(device_count, dtype=jnp.int32)).reshape(REQUESTS, D)
    merged = (residual.astype(jnp.float32) + attended.astype(jnp.float32)).astype(jnp.bfloat16)
    merged_wide = merged.astype(jnp.float32)
    normed = (merged_wide * lax.rsqrt(lax.optimization_barrier(jnp.mean(merged_wide * merged_wide, axis=-1, keepdims=True)) + epsilon) * norm_gain).astype(jnp.bfloat16)
    limit_rows = CAP * device_count

    def add_expert(running, inputs):
        gate_up, down_proj, expert = inputs
        matches = expert_ids == expert
        chosen = jnp.any(matches, axis=1)
        weight_rows = lax.optimization_barrier(jnp.sum(jnp.where(matches, gate_weights, 0.0), axis=1))
        selected = jnp.argsort(jnp.where(chosen, 0, 1).astype(jnp.int32), stable=True)[:limit_rows]
        output_rows = expert_rows(normed[selected], gate_up, down_proj).astype(jnp.float32)
        scaled = (weight_rows[selected] * chosen[selected].astype(jnp.float32))[:, None] * output_rows
        return (running.at[selected].add(scaled), None)
    expert_sum, ignored = lax.scan(add_expert, jnp.zeros((REQUESTS, D), jnp.float32), (w_gate_up, w_down, jnp.arange(EXPERTS, dtype=jnp.int32)))
    layer_out = (merged_wide + expert_sum).astype(jnp.bfloat16)
    return (attended, layer_out)
```

```python
import math

import jax
import jax.numpy as jnp
from jax import lax
from jax.experimental import pallas as pl
from jax.experimental.pallas import tpu as pltpu
from jax.sharding import PartitionSpec as P

HEAD_DIMENSION = 128
KEY_VALUE_HEADS = 2
QUERY_GROUP_SIZE = 16


masked_score = -1e30
epsilon = 1e-06


def from_behind(value, axis, by):
    length = lax.axis_size(axis)
    return lax.ppermute(value, axis, [(i, (i + by) % length) for i in range(length)])


def cache_scores(source, index_table, allowed, query_head_block, scaling):
    count_of_rows = index_table.shape[0]
    collected_rows = jnp.take(source, index_table, axis=0).reshape(
        count_of_rows, -1, source.shape[-1]
    )
    key_row_width = source.shape[-1] // 2
    group_heads = query_head_block.shape[1]
    head_size = query_head_block.shape[3]
    key_entries = collected_rows[:, :, :key_row_width].reshape(
        count_of_rows, -1, group_heads, head_size
    )
    value_entries = collected_rows[:, :, key_row_width:].reshape(
        count_of_rows, -1, group_heads, head_size
    )
    scores = (
        jnp.einsum(
            "rkgd,rlkd->rkgl", query_head_block, key_entries, preferred_element_type=jnp.float32
        )
        * scaling
    )
    scores = jnp.where(allowed[:, None, None, :], scores, masked_score)
    return (scores, value_entries)


def finish_attention(score_list, value_list, query_head_block, incoming_rows, scaling):
    count_of_rows = incoming_rows.shape[0]
    key_row_width = incoming_rows.shape[-1] // 2
    group_heads = query_head_block.shape[1]
    head_size = query_head_block.shape[3]
    incoming_keys = incoming_rows[:, :key_row_width].reshape(count_of_rows, group_heads, head_size)
    incoming_values = incoming_rows[:, key_row_width:].reshape(
        count_of_rows, group_heads, head_size
    )
    fresh_score = (
        jnp.einsum(
            "rkgd,rkd->rkg", query_head_block, incoming_keys, preferred_element_type=jnp.float32
        )
        * scaling
    )
    largest = fresh_score
    for scores in score_list:
        largest = jnp.maximum(largest, jnp.max(scores, axis=-1))
    fresh_weight = jnp.exp(fresh_score - largest)
    denominator = fresh_weight
    fresh_low = lax.optimization_barrier(fresh_weight.astype(jnp.bfloat16)).astype(jnp.float32)
    summed = fresh_low[..., None] * incoming_values.astype(jnp.float32)[:, :, None, :]
    for scores, value_entries in zip(score_list, value_list):
        weights = jnp.exp(scores - largest[..., None])
        denominator = denominator + jnp.sum(weights, axis=-1)
        summed = summed + jnp.einsum(
            "rkgl,rlkd->rkgd",
            weights.astype(jnp.bfloat16),
            value_entries,
            preferred_element_type=jnp.float32,
        )
    return (summed / denominator[..., None]).reshape(count_of_rows, -1).astype(jnp.bfloat16)


MESH_ID = pl.DeviceIdType.MESH
ROTATIONS = ((0, 1, 2), (1, 2, 0), (2, 0, 1))
SIDE = 4
PEERS = 8
CHUNKS = ((0, 0, 6), (1, 6, 5), (2, 11, 5), (0, 16, 5), (1, 21, 6), (2, 27, 5))


def coordinates():
    pool = lax.axis_index("pool")
    dev = lax.axis_index("dev")
    x = lax.div(dev, 16)
    y = lax.rem(lax.div(dev, 2), 4)
    z = pool * 2 + lax.rem(lax.div(dev, 8), 2)
    return (x, y, z), lax.rem(dev, 2)


def device_at(place, core):
    x, y, z = place
    return (lax.div(z, 2), x * 16 + lax.rem(z, 2) * 8 + y * 2 + core)


def shifted(place, axis, by):
    return tuple(
        lax.rem(value + by + SIDE, SIDE) if i == axis else value for i, value in enumerate(place)
    )


def routed_experts_kernel(
    normed, codes, merged, gate_up_hbm, down_hbm, out,
    gate_up, down, gathered, select, weight, first, packed, second, third, product, hidden,
    sent_back, back_one, back_two, partial, own_sum, back_three,
    w_sems, code_s, code_r, s1_s, s1_r, s2_s, s2_r, s3_s, s3_r, r3_s, r3_r, r2_s, r2_r, r1_s, r1_r,
):
    place, core = coordinates()
    hidden_dim = down.shape[0]
    loads = [
        pltpu.make_async_copy(gate_up_hbm, gate_up, w_sems.at[0]),
        pltpu.make_async_copy(down_hbm, down, w_sems.at[1]),
    ]
    for load in loads:
        load.start()

    def other(axis, by, flip):
        return device_at(shifted(place, axis, by), lax.rem(core + flip, 2))

    barrier = pltpu.get_barrier_semaphore()
    neighbours = [other(0, 0, 1)] + [
        other(axis, by, flip) for axis in range(3) for by in (1, 2, 3) for flip in (0, 1)
    ]
    for neighbour in neighbours:
        pl.semaphore_signal(barrier, inc=1, device_id=neighbour, device_id_type=MESH_ID)
    pl.semaphore_wait(barrier, len(neighbours))

    sends = []

    def send(source, target, send_sem, recv_sem, device):
        copy = pltpu.make_async_remote_copy(
            src_ref=source, dst_ref=target, send_sem=send_sem, recv_sem=recv_sem,
            device_id=device, device_id_type=MESH_ID,
        )
        copy.start()
        sends.append(copy)
        return copy

    def columns(start, count):
        return pl.ds(start * 128, count * 128)

    code_copies = []
    for i, (axis, by, flip) in enumerate(
        [(0, 0, 1)] + [(a, b, f) for a in range(3) for b in (1, 2, 3) for f in (0, 1)]
    ):
        code_copies.append(
            send(codes, gathered.at[i], code_s.at[i], code_r.at[i], other(axis, by, flip))
        )
    first_copies = []
    for c, (r, start, count) in enumerate(CHUNKS):
        axis = ROTATIONS[r][0]
        copies = []
        for s in range(1, PEERS):
            copies.append(
                send(
                    normed.at[:, columns(start, count)],
                    first.at[s, :, columns(start, count)],
                    s1_s.at[c, s], s1_r.at[c, s],
                    other(axis, s // 2, s % 2),
                )
            )
        first_copies.append(copies)
    first[0] = normed[...]
    for copy in code_copies:
        copy.wait_recv()

    row = lax.broadcasted_iota(jnp.int32, (256, 1), 0)
    lane = lax.broadcasted_iota(jnp.int32, (1, 128), 1)
    slot = lax.rem(row, 2)
    row_peer = lax.rem(lax.div(row, 2), PEERS)
    same_peer = row_peer == lax.div(lane, 16)
    lane_peer = lax.div(lax.broadcasted_iota(jnp.int32, (16, 128), 1), 16)
    for r, (a0, a1, a2) in enumerate(ROTATIONS):
        entries = jnp.where(lane_peer == 0, codes[...], 0.0)
        entries = jnp.where(lane_peer == 1, gathered[0], entries)
        for s in range(2, PEERS):
            entries = jnp.where(lane_peer == s, gathered[1 + a0 * 6 + s - 2], entries)
        where = list(place)
        where[a1] = lax.rem(place[a1] + lax.div(row, 64), SIDE)
        where[a2] = lax.rem(place[a2] + lax.rem(lax.div(row, 16), SIDE), SIDE)
        x, y, z = where
        expert = lax.div(z, 2) * 64 + x * 16 + lax.rem(z, 2) * 8 + y * 2 + core
        wanted = (expert * 2 + slot).astype(jnp.float32)
        chosen = jnp.zeros((256, 128), jnp.float32)
        gates = jnp.zeros((256, 128), jnp.float32)
        for k in range(8):
            match = same_peer & (entries[k : k + 1, :] == wanted)
            chosen = jnp.where(match, 1.0, chosen)
            gates = jnp.where(match, entries[8 + k : 9 + k, :], gates)
        select[r] = chosen.astype(jnp.bfloat16)
        for part in range(3):
            piece = gates.astype(jnp.bfloat16)
            weight[r, part] = piece
            gates = gates - piece.astype(jnp.float32)

    second_copies = []
    for c, (r, start, count) in enumerate(CHUNKS):
        a1 = ROTATIONS[r][1]
        for copy in first_copies[c]:
            copy.wait_recv()
        cols = columns(start, count)
        rows = first[:, :, cols].reshape(PEERS * 16, count * 128)
        block = jnp.dot(select[r], rows, preferred_element_type=jnp.float32).astype(jnp.bfloat16)
        block = block.reshape(SIDE, SIDE, 16, count * 128)
        second[0, :, :, cols] = block[0]
        copies = []
        for d in (2, 1, 3):
            packed[d, :, :, cols] = block[d]
        for d in (2, 1, 3):
            copies.append(
                send(
                    packed.at[d, :, :, cols], second.at[d, :, :, cols],
                    s2_s.at[c, d], s2_r.at[c, d], other(a1, d, 0),
                )
            )
        second_copies.append(copies)
    third_copies = []
    for c, (r, start, count) in enumerate(CHUNKS):
        a2 = ROTATIONS[r][2]
        for copy in second_copies[c]:
            copy.wait_recv()
        cols = columns(start, count)
        copies = []
        for d in (2, 1, 3):
            copies.append(
                send(
                    second.at[:, d, :, cols], third.at[d, :, :, cols],
                    s3_s.at[c, d], s3_r.at[c, d], other(a2, d, 0),
                )
            )
        third[0, :, :, cols] = second[:, 0, :, cols]
        third_copies.append(copies)

    canon = lax.broadcasted_iota(jnp.int32, (256, 256), 0)
    local = lax.broadcasted_iota(jnp.int32, (256, 256), 1)
    apart = (
        lax.rem(lax.div(canon, 4), SIDE),
        lax.rem(lax.div(canon, 16), SIDE),
        lax.div(canon, 64),
    )
    orders = []
    for a0, a1, a2 in ROTATIONS:
        index = apart[a2] * 64 + apart[a1] * 16 + apart[a0] * 4 + lax.rem(canon, 4)
        orders.append((index == local).astype(jnp.bfloat16))

    loads[0].wait()
    for c, (r, start, count) in enumerate(CHUNKS):
        for copy in third_copies[c]:
            copy.wait_recv()
        cols = columns(start, count)
        tokens = third[:, :, :, cols].reshape(256, count * 128)
        if r:
            tokens = jnp.dot(orders[r], tokens, preferred_element_type=jnp.float32)
            tokens = tokens.astype(jnp.bfloat16)
        for n in range(0, 2 * hidden_dim, 512):
            piece = jnp.dot(
                tokens, gate_up[pl.ds(start * 128, count * 128), pl.ds(n, 512)],
                preferred_element_type=jnp.float32,
            )
            if c:
                piece = product[:, pl.ds(n, 512)] + piece
            product[:, pl.ds(n, 512)] = piece
    gate = product[:, :hidden_dim]
    active = (gate / (1.0 + jnp.exp(-gate)) * product[:, hidden_dim:]).astype(jnp.bfloat16)
    hidden[0] = active
    for r in (1, 2):
        turned = lax.dot_general(
            orders[r], active, (((0,), (0,)), ((), ())), preferred_element_type=jnp.float32
        )
        hidden[r] = turned.astype(jnp.bfloat16)

    loads[1].wait()
    one_copies = []
    for c, (r, start, count) in enumerate(CHUNKS):
        a2 = ROTATIONS[r][2]
        cols = columns(start, count)
        finished = jnp.dot(hidden[r], down[:, cols], preferred_element_type=jnp.float32)
        finished = finished.astype(jnp.bfloat16).reshape(SIDE, SIDE, 16, count * 128)
        back_one[0, :, :, cols] = finished[0]
        for d in (2, 1, 3):
            sent_back[d, :, :, cols] = finished[d]
        copies = []
        for d in (2, 1, 3):
            copies.append(
                send(
                    sent_back.at[d, :, :, cols], back_one.at[d, :, :, cols],
                    r3_s.at[c, d], r3_r.at[c, d], other(a2, -d, 0),
                )
            )
        one_copies.append(copies)
    two_copies = []
    for c, (r, start, count) in enumerate(CHUNKS):
        a1 = ROTATIONS[r][1]
        for copy in one_copies[c]:
            copy.wait_recv()
        cols = columns(start, count)
        copies = []
        for d in (2, 1, 3):
            copies.append(
                send(
                    back_one.at[:, d, :, cols], back_two.at[d, :, :, cols],
                    r2_s.at[c, d], r2_r.at[c, d], other(a1, -d, 0),
                )
            )
        back_two[0, :, :, cols] = back_one[:, 0, :, cols]
        two_copies.append(copies)
    three_copies = []
    for c, (r, start, count) in enumerate(CHUNKS):
        a0 = ROTATIONS[r][0]
        for copy in two_copies[c]:
            copy.wait_recv()
        cols = columns(start, count)
        results = back_two[:, :, :, cols].reshape(256, count * 128)
        total = None
        for part in range(3):
            piece = lax.dot_general(
                weight[r, part], results, (((0,), (0,)), ((), ())),
                preferred_element_type=jnp.float32,
            )
            total = piece if total is None else total + piece
        total = total.reshape(PEERS, 16, count * 128)
        own_sum[:, cols] = total[0]
        partial[1:, :, cols] = total[1:].astype(jnp.bfloat16)
        copies = []
        for s in range(1, PEERS):
            copies.append(
                send(
                    partial.at[s, :, cols], back_three.at[s, :, cols],
                    r1_s.at[c, s], r1_r.at[c, s], other(a0, -(s // 2), s % 2),
                )
            )
        three_copies.append(copies)
    for c, (r, start, count) in enumerate(CHUNKS):
        for copy in three_copies[c]:
            copy.wait_recv()
        cols = columns(start, count)
        total = own_sum[:, cols]
        for s in range(1, PEERS):
            total = total + back_three[s, :, cols].astype(jnp.float32)
        out[:, cols] = (merged[:, cols].astype(jnp.float32) + total).astype(jnp.bfloat16)
    for copy in sends:
        copy.wait_send()


def routed_experts(normed, codes, merged, gate_up, down):
    width = normed.shape[1]
    hidden_dim = down.shape[0]
    chunks = len(CHUNKS)
    bf16, f32 = jnp.bfloat16, jnp.float32
    vmem = pl.BlockSpec(memory_space=pltpu.VMEM)
    hbm = pl.BlockSpec(memory_space=pl.ANY)
    block = pltpu.VMEM((SIDE, SIDE, 16, width), bf16)
    peers = pltpu.VMEM((PEERS, 16, width), bf16)
    dma = pltpu.SemaphoreType.DMA
    return pl.pallas_call(
        routed_experts_kernel,
        out_shape=jax.ShapeDtypeStruct(normed.shape, bf16),
        in_specs=[vmem, vmem, vmem, hbm, hbm],
        out_specs=vmem,
        scratch_shapes=[
            pltpu.VMEM(gate_up.shape, bf16),
            pltpu.VMEM(down.shape, bf16),
            pltpu.VMEM((19, 16, 128), f32),
            pltpu.VMEM((3, 256, 128), bf16),
            pltpu.VMEM((3, 3, 256, 128), bf16),
            peers,
            block,
            block,
            block,
            pltpu.VMEM((256, 2 * hidden_dim), f32),
            pltpu.VMEM((3, 256, hidden_dim), bf16),
            block,
            block,
            block,
            peers,
            pltpu.VMEM((16, width), f32),
            peers,
            dma((2,)),
            dma((19,)), dma((19,)),
            dma((chunks, PEERS)), dma((chunks, PEERS)),
            dma((chunks, SIDE)), dma((chunks, SIDE)),
            dma((chunks, SIDE)), dma((chunks, SIDE)),
            dma((chunks, SIDE)), dma((chunks, SIDE)),
            dma((chunks, SIDE)), dma((chunks, SIDE)),
            dma((chunks, PEERS)), dma((chunks, PEERS)),
        ],
        compiler_params=pltpu.CompilerParams(
            collective_id=0, has_side_effects=True, vmem_limit_bytes=60 * 1024 * 1024
        ),
    )(normed, codes, merged, gate_up, down)


def local(
    queries,
    new_kv,
    kv_pages,
    page_table,
    lengths,
    shed_slots,
    residual,
    norm_gain,
    expert_ids,
    gate_weights,
    w_gate_up,
    w_down,
):
    count_of_rows, model_dim = queries.shape
    pages_own, page_len, kv_width = kv_pages.shape
    table_width = page_table.shape[1]
    query_head_block = queries.reshape(
        count_of_rows, KEY_VALUE_HEADS, QUERY_GROUP_SIZE, HEAD_DIMENSION
    )
    scaling = 1.0 / math.sqrt(HEAD_DIMENSION)
    positions = jnp.arange(table_width * page_len, dtype=jnp.int32)
    allowed = positions[None, :] < lengths[:, None]
    requested = from_behind(shed_slots, "pool", 1)
    fetched = from_behind(jnp.take(kv_pages, requested, axis=0), "pool", 1)
    combined = jnp.concatenate([kv_pages, fetched], axis=0)
    scores, value_entries = cache_scores(combined, page_table, allowed, query_head_block, scaling)
    attended = finish_attention([scores], [value_entries], query_head_block, new_kv, scaling)
    merged = (residual.astype(jnp.float32) + attended.astype(jnp.float32)).astype(jnp.bfloat16)
    merged_wide = merged.astype(jnp.float32)
    normed = (
        merged_wide
        * lax.rsqrt(jnp.mean(merged_wide * merged_wide, axis=-1, keepdims=True) + epsilon)
        * norm_gain
    ).astype(jnp.bfloat16)
    same = expert_ids[:, :, None, None] == expert_ids[None, None, :, :]
    row_index = jnp.arange(count_of_rows, dtype=jnp.int32)
    before = row_index[:, None, None, None] > row_index[None, None, :, None]
    slot_rank = jnp.sum((same & before).astype(jnp.int32), axis=(2, 3))
    codes = jnp.concatenate(
        [(expert_ids * 2 + slot_rank).astype(jnp.float32).T, gate_weights.T], axis=0
    )
    codes = jnp.tile(codes, (1, PEERS))
    layer_out = routed_experts(normed, codes, merged, w_gate_up[0], w_down[0])
    return (attended, layer_out)


def solution(mesh):
    return jax.shard_map(
        local,
        mesh=mesh,
        in_specs=(
            P(("pool", "dev"), None),
            P(("pool", "dev"), None),
            P(("pool", "dev"), None, None),
            P(("pool", "dev"), None),
            P(("pool", "dev")),
            P(("pool", "dev")),
            P(("pool", "dev"), None),
            P(),
            P(("pool", "dev"), None),
            P(("pool", "dev"), None),
            P(("pool", "dev"), None, None),
            P(("pool", "dev"), None, None),
        ),
        out_specs=(P(("pool", "dev"), None), P(("pool", "dev"), None)),
        check_vma=False,
    )
```

```python
import math

import jax
import jax.numpy as jnp
from jax import lax
from jax.experimental import pallas as pl
from jax.experimental.pallas import tpu as pltpu
from jax.sharding import PartitionSpec as P

HEAD = 128
GROUPS = 2
GROUP_HEADS = 16
ROWS = 16
PAGE = 16
TILE_PAGES = 16
TILE = TILE_PAGES * PAGE
EXTRA = 128

masked_score = -1e30
epsilon = 1e-06

MESH_ID = pl.DeviceIdType.MESH
ROTATIONS = ((0, 1, 2), (1, 2, 0), (2, 0, 1))
SIDE = 4
PEERS = 8
CHUNKS = ((0, 0, 6), (1, 6, 5), (2, 11, 5), (0, 16, 5), (1, 21, 6), (2, 27, 5))


def coordinates():
    pool = lax.axis_index("pool")
    dev = lax.axis_index("dev")
    x = lax.div(dev, 16)
    y = lax.rem(lax.div(dev, 2), 4)
    z = pool * 2 + lax.rem(lax.div(dev, 8), 2)
    return (x, y, z), lax.rem(dev, 2)


def device_at(place, core):
    x, y, z = place
    return (lax.div(z, 2), x * 16 + lax.rem(z, 2) * 8 + y * 2 + core)


def shifted(place, axis, by):
    return tuple(
        lax.rem(value + by + SIDE, SIDE) if i == axis else value for i, value in enumerate(place)
    )


def layer_kernel(
    queries, new_kv, pages_hbm, page_table, lengths, shed_list, residual, gain, ids, gate_in,
    gate_up_hbm, down_hbm, attended, merged, expert_sum,
    pages, extra, wanted_list, wanted_scalar, shed_out, shed_in, heads, scores, extra_scores,
    peak, weight_sum, summed, normed, codes,
    gate_up, down, gathered, select, weight, first, packed, second, third, product, hidden,
    sent_back, back_one, back_two, partial, back_three,
    w_sems, shed_sems, code_s, code_r, s1_s, s1_r, s2_s, s2_r, s3_s, s3_r,
    r3_s, r3_r, r2_s, r2_r, r1_s, r1_r,
):
    bf16, f32 = jnp.bfloat16, jnp.float32
    place, core = coordinates()
    hidden_dim = down.shape[0]
    own_pages = pages_hbm.shape[0]
    load_pages = pltpu.make_async_copy(pages_hbm, pages, w_sems.at[2])
    load_pages.start()

    def other(axis, by, flip):
        return device_at(shifted(place, axis, by), lax.rem(core + flip, 2))

    barrier = pltpu.get_barrier_semaphore()
    neighbours = [other(0, 0, 1)] + [
        other(axis, by, flip) for axis in range(3) for by in (1, 2, 3) for flip in (0, 1)
    ]
    for neighbour in neighbours:
        pl.semaphore_signal(barrier, inc=1, device_id=neighbour, device_id_type=MESH_ID)
    pl.semaphore_wait(barrier, len(neighbours))

    sends = []

    def send(source, target, send_sem, recv_sem, device):
        copy = pltpu.make_async_remote_copy(
            src_ref=source, dst_ref=target, send_sem=send_sem, recv_sem=recv_sem,
            device_id=device, device_id_type=MESH_ID,
        )
        copy.start()
        sends.append(copy)
        return copy

    def columns(start, count):
        return pl.ds(start * 128, count * 128)

    partner = other(2, 2, 0)
    list_copy = send(shed_list, wanted_list, shed_sems.at[0], shed_sems.at[1], partner)
    loads = [
        pltpu.make_async_copy(gate_up_hbm, gate_up, w_sems.at[0]),
        pltpu.make_async_copy(down_hbm, down, w_sems.at[1]),
    ]

    lane16 = lax.rem(lax.broadcasted_iota(jnp.int32, (16, 128), 1), 16)
    sub16 = lax.broadcasted_iota(jnp.int32, (16, 128), 0)
    repeat = (lane16 == sub16).astype(bf16)
    earlier = (sub16 < lane16).astype(bf16)
    own_ids = ids[...].astype(f32)
    id_rows = jnp.dot(own_ids.astype(bf16), repeat, preferred_element_type=f32)
    gates_left = gate_in[...]
    gate_rows = None
    for _ in range(3):
        piece = gates_left.astype(bf16)
        term = jnp.dot(piece, repeat, preferred_element_type=f32)
        gate_rows = term if gate_rows is None else gate_rows + term
        gates_left = gates_left - piece.astype(f32)
    expert_sub = lax.broadcasted_iota(jnp.int32, (128, 1), 0).astype(f32)
    member = jnp.zeros((128, 16), f32)
    for k in range(8):
        member = jnp.where(own_ids[k : k + 1, :] == expert_sub, 1.0, member)
    before = jnp.dot(member.astype(bf16), earlier, preferred_element_type=f32)
    for k in range(8):
        rank = jnp.sum(
            jnp.where(id_rows[k : k + 1, :] == expert_sub, before, 0.0), axis=0, keepdims=True
        )
        codes[k : k + 1, :] = id_rows[k : k + 1, :] * 2.0 + rank
    codes[8:16, :] = gate_rows
    code_copies = []
    for i, (axis, by, flip) in enumerate(
        [(0, 0, 1)] + [(a, b, f) for a in range(3) for b in (1, 2, 3) for f in (0, 1)]
    ):
        code_copies.append(
            send(codes, gathered.at[i], code_s.at[i], code_r.at[i], other(axis, by, flip))
        )

    load_pages.wait()
    for load in loads:
        load.start()
    list_copy.wait_recv()
    to_scalar = pltpu.make_async_copy(wanted_list, wanted_scalar, w_sems.at[3])
    to_scalar.start()
    to_scalar.wait()
    shed_copies = []
    half = shed_out.shape[0] // 2
    for part in range(2):
        for i in range(part * half, part * half + half):
            shed_out[i] = pages[wanted_scalar[0, i]]
        span = pl.ds(part * half, half)
        shed_copies.append(
            send(
                shed_out.at[span], shed_in.at[span],
                shed_sems.at[2 + part], shed_sems.at[4 + part], partner,
            )
        )

    scaling = 1.0 / math.sqrt(HEAD)
    for g in range(GROUPS):
        for h in range(GROUP_HEADS):
            heads[g, h * ROWS : (h + 1) * ROWS, :] = queries[
                :, (g * GROUP_HEADS + h) * HEAD : (g * GROUP_HEADS + h + 1) * HEAD
            ]
    extra[...] = jnp.zeros_like(extra)
    extra[0:ROWS, :] = new_kv[...]
    table = page_table[...].astype(f32)
    diagonal = lax.broadcasted_iota(jnp.int32, (ROWS, ROWS), 0) == lax.broadcasted_iota(
        jnp.int32, (ROWS, ROWS), 1
    )
    length = jnp.sum(
        jnp.where(diagonal, lengths[...].astype(f32), 0.0), axis=1, keepdims=True
    )
    token = lax.broadcasted_iota(jnp.int32, (ROWS, TILE), 1)
    token_page = lax.div(token, PAGE).astype(f32)
    token_place = lax.rem(token, PAGE).astype(f32)

    def allowed(first_page):
        limit = jnp.zeros((ROWS, TILE), f32)
        for j in range(table.shape[1]):
            left = jnp.maximum(length - float(j * PAGE), 0.0)
            limit = limit + jnp.where(table[:, j : j + 1] == token_page + first_page, left, 0.0)
        return token_place < limit

    def masked(values, mask):
        width = values.shape[1]
        values = values.reshape(GROUP_HEADS, ROWS, width)
        return jnp.where(mask[None], values, masked_score).reshape(GROUP_HEADS * ROWS, width)

    def dot_last(left, right):
        return lax.dot_general(
            left, right, (((1,), (1,)), ((), ())), preferred_element_type=f32
        )

    new_mask = lax.broadcasted_iota(jnp.int32, (ROWS, EXTRA), 0) == lax.broadcasted_iota(
        jnp.int32, (ROWS, EXTRA), 1
    )
    for g in range(GROUPS):
        keys = extra[:, g * HEAD : (g + 1) * HEAD]
        values = masked(dot_last(heads[g], keys), new_mask)
        extra_scores[g] = values
        peak[g] = values
    tiles = own_pages // TILE_PAGES

    def score_tile(t, carry):
        mask = allowed((t * TILE_PAGES).astype(f32))
        for g in range(GROUPS):
            keys = pages[pl.ds(t * TILE_PAGES, TILE_PAGES), :, g * HEAD : (g + 1) * HEAD]
            values = masked(dot_last(heads[g], keys.reshape(TILE, HEAD)), mask)
            scores[g, t] = values
            peak[g] = jnp.maximum(peak[g], jnp.maximum(values[:, :128], values[:, 128:]))
        return carry

    lax.fori_loop(0, tiles, score_tile, 0)
    tops = []
    for g in range(GROUPS):
        top = jnp.max(peak[g], axis=1, keepdims=True)
        tops.append(top)
        weights = jnp.exp((extra_scores[g] - top) * scaling)
        weight_sum[g] = weights
        values = extra[:, (GROUPS + g) * HEAD : (GROUPS + g + 1) * HEAD]
        summed[g] = jnp.dot(weights.astype(bf16), values, preferred_element_type=f32)

    def weigh_tile(t, carry):
        for g in range(GROUPS):
            weights = jnp.exp((scores[g, t] - tops[g]) * scaling)
            weight_sum[g] += weights[:, :128] + weights[:, 128:]
            values = pages[
                pl.ds(t * TILE_PAGES, TILE_PAGES), :, (GROUPS + g) * HEAD : (GROUPS + g + 1) * HEAD
            ]
            summed[g] += jnp.dot(
                weights.astype(bf16), values.reshape(TILE, HEAD), preferred_element_type=f32
            )
        return carry

    lax.fori_loop(0, tiles, weigh_tile, 0)
    sums = [jnp.sum(weight_sum[g], axis=1, keepdims=True) for g in range(GROUPS)]

    for copy in code_copies:
        copy.wait_recv()

    row = lax.broadcasted_iota(jnp.int32, (256, 1), 0)
    lane = lax.broadcasted_iota(jnp.int32, (1, 128), 1)
    slot = lax.rem(row, 2)
    row_peer = lax.rem(lax.div(row, 2), PEERS)
    same_peer = row_peer == lax.div(lane, 16)
    lane_peer = lax.div(lax.broadcasted_iota(jnp.int32, (16, 128), 1), 16)
    for r, (a0, a1, a2) in enumerate(ROTATIONS):
        entries = jnp.where(lane_peer == 0, codes[...], 0.0)
        entries = jnp.where(lane_peer == 1, gathered[0], entries)
        for s in range(2, PEERS):
            entries = jnp.where(lane_peer == s, gathered[1 + a0 * 6 + s - 2], entries)
        where = list(place)
        where[a1] = lax.rem(place[a1] + lax.div(row, 64), SIDE)
        where[a2] = lax.rem(place[a2] + lax.rem(lax.div(row, 16), SIDE), SIDE)
        x, y, z = where
        expert = lax.div(z, 2) * 64 + x * 16 + lax.rem(z, 2) * 8 + y * 2 + core
        wanted = (expert * 2 + slot).astype(jnp.float32)
        chosen = jnp.zeros((256, 128), jnp.float32)
        gates = jnp.zeros((256, 128), jnp.float32)
        for k in range(8):
            match = same_peer & (entries[k : k + 1, :] == wanted)
            chosen = jnp.where(match, 1.0, chosen)
            gates = jnp.where(match, entries[8 + k : 9 + k, :], gates)
        select[r] = chosen.astype(jnp.bfloat16)
        for part in range(3):
            piece = gates.astype(jnp.bfloat16)
            weight[r, part] = piece
            gates = gates - piece.astype(jnp.float32)


    shed_mask = allowed(float(own_pages))
    for copy in shed_copies:
        copy.wait_recv()
    square = jnp.zeros((ROWS, HEAD), f32)
    for g in range(GROUPS):
        keys = shed_in[:, :, g * HEAD : (g + 1) * HEAD].reshape(TILE, HEAD)
        values = masked(dot_last(heads[g], keys), shed_mask)
        top = jnp.maximum(tops[g], jnp.max(values, axis=1, keepdims=True))
        again = jnp.exp((tops[g] - top) * scaling)
        weights = jnp.exp((values - top) * scaling)
        denominator = sums[g] * again + jnp.sum(weights, axis=1, keepdims=True)
        values = shed_in[:, :, (GROUPS + g) * HEAD : (GROUPS + g + 1) * HEAD].reshape(TILE, HEAD)
        total = summed[g] * again + jnp.dot(
            weights.astype(bf16), values, preferred_element_type=f32
        )
        total = (total / denominator).astype(bf16)
        for h in range(GROUP_HEADS):
            span = pl.ds((g * GROUP_HEADS + h) * HEAD, HEAD)
            part = total[h * ROWS : (h + 1) * ROWS, :]
            attended[:, span] = part
            joined = (residual[:, span].astype(f32) + part.astype(f32)).astype(bf16)
            merged[:, span] = joined
            joined = joined.astype(f32)
            square = square + joined * joined
    width = queries.shape[1]
    mean = jnp.sum(square, axis=1, keepdims=True) * (1.0 / width)
    inverse = lax.rsqrt(mean + epsilon)
    normed[...] = (merged[...].astype(f32) * inverse * gain[...]).astype(bf16)

    first_copies = []
    for c, (r, start, count) in enumerate(CHUNKS):
        axis = ROTATIONS[r][0]
        copies = []
        for s in range(1, PEERS):
            copies.append(
                send(
                    normed.at[:, columns(start, count)],
                    first.at[s, :, columns(start, count)],
                    s1_s.at[c, s], s1_r.at[c, s],
                    other(axis, s // 2, s % 2),
                )
            )
        first_copies.append(copies)
    first[0] = normed[...]
    second_copies = []
    for c, (r, start, count) in enumerate(CHUNKS):
        a1 = ROTATIONS[r][1]
        for copy in first_copies[c]:
            copy.wait_recv()
        cols = columns(start, count)
        rows = first[:, :, cols].reshape(PEERS * 16, count * 128)
        block = jnp.dot(select[r], rows, preferred_element_type=jnp.float32).astype(jnp.bfloat16)
        block = block.reshape(SIDE, SIDE, 16, count * 128)
        second[0, :, :, cols] = block[0]
        copies = []
        for d in (2, 1, 3):
            packed[d, :, :, cols] = block[d]
        for d in (2, 1, 3):
            copies.append(
                send(
                    packed.at[d, :, :, cols], second.at[d, :, :, cols],
                    s2_s.at[c, d], s2_r.at[c, d], other(a1, d, 0),
                )
            )
        second_copies.append(copies)
    third_copies = []
    for c, (r, start, count) in enumerate(CHUNKS):
        a2 = ROTATIONS[r][2]
        for copy in second_copies[c]:
            copy.wait_recv()
        cols = columns(start, count)
        copies = []
        for d in (2, 1, 3):
            copies.append(
                send(
                    second.at[:, d, :, cols], third.at[d, :, :, cols],
                    s3_s.at[c, d], s3_r.at[c, d], other(a2, d, 0),
                )
            )
        third[0, :, :, cols] = second[:, 0, :, cols]
        third_copies.append(copies)

    canon = lax.broadcasted_iota(jnp.int32, (256, 256), 0)
    local = lax.broadcasted_iota(jnp.int32, (256, 256), 1)
    apart = (
        lax.rem(lax.div(canon, 4), SIDE),
        lax.rem(lax.div(canon, 16), SIDE),
        lax.div(canon, 64),
    )
    orders = []
    for a0, a1, a2 in ROTATIONS:
        index = apart[a2] * 64 + apart[a1] * 16 + apart[a0] * 4 + lax.rem(canon, 4)
        orders.append((index == local).astype(jnp.bfloat16))

    loads[0].wait()
    for c, (r, start, count) in enumerate(CHUNKS):
        for copy in third_copies[c]:
            copy.wait_recv()
        cols = columns(start, count)
        tokens = third[:, :, :, cols].reshape(256, count * 128)
        if r:
            tokens = jnp.dot(orders[r], tokens, preferred_element_type=jnp.float32)
            tokens = tokens.astype(jnp.bfloat16)
        for n in range(0, 2 * hidden_dim, 512):
            piece = jnp.dot(
                tokens, gate_up[pl.ds(start * 128, count * 128), pl.ds(n, 512)],
                preferred_element_type=jnp.float32,
            )
            if c:
                piece = product[:, pl.ds(n, 512)] + piece
            product[:, pl.ds(n, 512)] = piece
    gate = product[:, :hidden_dim]
    active = (gate / (1.0 + jnp.exp(-gate)) * product[:, hidden_dim:]).astype(jnp.bfloat16)
    hidden[0] = active
    for r in (1, 2):
        turned = lax.dot_general(
            orders[r], active, (((0,), (0,)), ((), ())), preferred_element_type=jnp.float32
        )
        hidden[r] = turned.astype(jnp.bfloat16)

    loads[1].wait()
    one_copies = []
    for c, (r, start, count) in enumerate(CHUNKS):
        a2 = ROTATIONS[r][2]
        cols = columns(start, count)
        finished = jnp.dot(hidden[r], down[:, cols], preferred_element_type=jnp.float32)
        finished = finished.astype(jnp.bfloat16).reshape(SIDE, SIDE, 16, count * 128)
        back_one[0, :, :, cols] = finished[0]
        for d in (2, 1, 3):
            sent_back[d, :, :, cols] = finished[d]
        copies = []
        for d in (2, 1, 3):
            copies.append(
                send(
                    sent_back.at[d, :, :, cols], back_one.at[d, :, :, cols],
                    r3_s.at[c, d], r3_r.at[c, d], other(a2, -d, 0),
                )
            )
        one_copies.append(copies)
    two_copies = []
    for c, (r, start, count) in enumerate(CHUNKS):
        a1 = ROTATIONS[r][1]
        for copy in one_copies[c]:
            copy.wait_recv()
        cols = columns(start, count)
        copies = []
        for d in (2, 1, 3):
            copies.append(
                send(
                    back_one.at[:, d, :, cols], back_two.at[d, :, :, cols],
                    r2_s.at[c, d], r2_r.at[c, d], other(a1, -d, 0),
                )
            )
        back_two[0, :, :, cols] = back_one[:, 0, :, cols]
        two_copies.append(copies)
    three_copies = []
    for c, (r, start, count) in enumerate(CHUNKS):
        a0 = ROTATIONS[r][0]
        for copy in two_copies[c]:
            copy.wait_recv()
        cols = columns(start, count)
        results = back_two[:, :, :, cols].reshape(256, count * 128)
        total = None
        for part in range(3):
            piece = lax.dot_general(
                weight[r, part], results, (((0,), (0,)), ((), ())),
                preferred_element_type=jnp.float32,
            )
            total = piece if total is None else total + piece
        total = total.reshape(PEERS, 16, count * 128)
        expert_sum[:, cols] = total[0]
        partial[1:, :, cols] = total[1:].astype(jnp.bfloat16)
        copies = []
        for s in range(1, PEERS):
            copies.append(
                send(
                    partial.at[s, :, cols], back_three.at[s, :, cols],
                    r1_s.at[c, s], r1_r.at[c, s], other(a0, -(s // 2), s % 2),
                )
            )
        three_copies.append(copies)
    for c, (r, start, count) in enumerate(CHUNKS):
        for copy in three_copies[c]:
            copy.wait_recv()
        cols = columns(start, count)
        total = expert_sum[:, cols]
        for s in range(1, PEERS):
            total = total + back_three[s, :, cols].astype(jnp.float32)
        expert_sum[:, cols] = total
    for copy in sends:
        copy.wait_send()


def local(
    queries, new_kv, kv_pages, page_table, lengths, shed_slots, residual, norm_gain,
    expert_ids, gate_weights, w_gate_up, w_down,
):
    rows, width = queries.shape
    gate_up, down = w_gate_up[0], w_down[0]
    hidden_dim = down.shape[0]
    pages, page, kv_width = kv_pages.shape
    shed = shed_slots.shape[0]
    chunks = len(CHUNKS)
    bf16, f32 = jnp.bfloat16, jnp.float32
    vmem = pl.BlockSpec(memory_space=pltpu.VMEM)
    hbm = pl.BlockSpec(memory_space=pl.ANY)
    block = pltpu.VMEM((SIDE, SIDE, 16, width), bf16)
    peers = pltpu.VMEM((PEERS, 16, width), bf16)
    dma = pltpu.SemaphoreType.DMA
    group_rows = GROUP_HEADS * ROWS
    attended, merged, expert_sum = pl.pallas_call(
        layer_kernel,
        out_shape=(
            jax.ShapeDtypeStruct((rows, width), bf16),
            jax.ShapeDtypeStruct((rows, width), bf16),
            jax.ShapeDtypeStruct((rows, width), f32),
        ),
        in_specs=[vmem, vmem, hbm, vmem, vmem, vmem, vmem, vmem, vmem, vmem, hbm, hbm],
        out_specs=(vmem, vmem, vmem),
        scratch_shapes=[
            pltpu.VMEM((pages, page, kv_width), bf16),
            pltpu.VMEM((EXTRA, kv_width), bf16),
            pltpu.VMEM((1, shed), jnp.int32),
            pltpu.SMEM((1, shed), jnp.int32),
            pltpu.VMEM((shed, page, kv_width), bf16),
            pltpu.VMEM((shed, page, kv_width), bf16),
            pltpu.VMEM((GROUPS, group_rows, HEAD), bf16),
            pltpu.VMEM((GROUPS, pages // TILE_PAGES, group_rows, TILE), f32),
            pltpu.VMEM((GROUPS, group_rows, EXTRA), f32),
            pltpu.VMEM((GROUPS, group_rows, 128), f32),
            pltpu.VMEM((GROUPS, group_rows, 128), f32),
            pltpu.VMEM((GROUPS, group_rows, HEAD), f32),
            pltpu.VMEM((rows, width), bf16),
            pltpu.VMEM((16, 128), f32),
            pltpu.VMEM(gate_up.shape, bf16),
            pltpu.VMEM(down.shape, bf16),
            pltpu.VMEM((19, 16, 128), f32),
            pltpu.VMEM((3, 256, 128), bf16),
            pltpu.VMEM((3, 3, 256, 128), bf16),
            peers,
            block,
            block,
            block,
            pltpu.VMEM((256, 2 * hidden_dim), f32),
            pltpu.VMEM((3, 256, hidden_dim), bf16),
            block,
            block,
            block,
            peers,
            peers,
            dma((4,)),
            dma((6,)),
            dma((19,)), dma((19,)),
            dma((chunks, PEERS)), dma((chunks, PEERS)),
            dma((chunks, SIDE)), dma((chunks, SIDE)),
            dma((chunks, SIDE)), dma((chunks, SIDE)),
            dma((chunks, SIDE)), dma((chunks, SIDE)),
            dma((chunks, SIDE)), dma((chunks, SIDE)),
            dma((chunks, PEERS)), dma((chunks, PEERS)),
        ],
        compiler_params=pltpu.CompilerParams(
            collective_id=0, has_side_effects=True, vmem_limit_bytes=60 * 1024 * 1024
        ),
    )(
        queries, new_kv, kv_pages, page_table, lengths.reshape(1, rows),
        shed_slots.reshape(1, shed), residual, norm_gain.reshape(1, width),
        expert_ids.T, gate_weights.T, gate_up, down,
    )
    layer_out = (merged.astype(f32) + expert_sum).astype(bf16)
    return (attended, layer_out)


def solution(mesh):
    return jax.shard_map(
        local,
        mesh=mesh,
        in_specs=(
            P(("pool", "dev"), None),
            P(("pool", "dev"), None),
            P(("pool", "dev"), None, None),
            P(("pool", "dev"), None),
            P(("pool", "dev")),
            P(("pool", "dev")),
            P(("pool", "dev"), None),
            P(),
            P(("pool", "dev"), None),
            P(("pool", "dev"), None),
            P(("pool", "dev"), None, None),
            P(("pool", "dev"), None, None),
        ),
        out_specs=(P(("pool", "dev"), None), P(("pool", "dev"), None)),
        check_vma=False,
    )
```

```python
import math

import jax
import jax.numpy as jnp
from jax import lax
from jax.experimental import pallas as pl
from jax.experimental.pallas import tpu as pltpu
from jax.sharding import PartitionSpec as P

HEAD = 128
GROUPS = 2
GROUP_HEADS = 16
ROWS = 16
PAGE = 16
TILE_PAGES = 16
TILE = TILE_PAGES * PAGE
EXTRA = 128

masked_score = -1e30
epsilon = 1e-06

MESH_ID = pl.DeviceIdType.MESH
ROTATIONS = ((0, 1, 2), (1, 2, 0), (2, 0, 1))
SIDE = 4
PEERS = 8
CHUNKS = ((0, 0, 6), (1, 6, 5), (2, 11, 5), (0, 16, 5), (1, 21, 6), (2, 27, 5))


def coordinates():
    pool = lax.axis_index("pool")
    dev = lax.axis_index("dev")
    x = lax.div(dev, 16)
    y = lax.rem(lax.div(dev, 2), 4)
    z = pool * 2 + lax.rem(lax.div(dev, 8), 2)
    return (x, y, z), lax.rem(dev, 2)


def device_at(place, core):
    x, y, z = place
    return (lax.div(z, 2), x * 16 + lax.rem(z, 2) * 8 + y * 2 + core)


def shifted(place, axis, by):
    return tuple(
        lax.rem(value + by + SIDE, SIDE) if i == axis else value for i, value in enumerate(place)
    )


def layer_kernel(
    queries_hbm, new_kv_hbm, pages_hbm, page_table_hbm, lengths_hbm, shed_list, residual_hbm,
    gain_hbm, ids_hbm, gate_in_hbm, gate_up_hbm, down_hbm, attended_out, layer_out,
    queries, new_kv, page_table, lengths, residual, gain, ids, gate_in,
    attended, merged, expert_sum,
    pages, extra, wanted_list, wanted_scalar, shed_out, shed_in, heads, scores, extra_scores,
    peak, weight_sum, summed, normed, codes,
    gate_up, down, gathered, select, weight, first, packed, second, third, product, hidden,
    sent_back, back_one, back_two, partial, back_three,
    w_sems, in_sems, shed_sems, code_sems, sent, s1_r, s2_r, s3_r, r3_r, r2_r, r1_r,
):
    bf16, f32 = jnp.bfloat16, jnp.float32
    place, core = coordinates()
    hidden_dim = down.shape[0]
    own_pages = pages_hbm.shape[0]
    load_pages = pltpu.make_async_copy(pages_hbm, pages, w_sems.at[2])
    inputs = []
    for i, (source, target) in enumerate(
        (
            (ids_hbm, ids), (gate_in_hbm, gate_in), (page_table_hbm, page_table),
            (lengths_hbm, lengths), (queries_hbm, queries), (new_kv_hbm, new_kv),
            (residual_hbm, residual), (gain_hbm, gain),
        )
    ):
        inputs.append(pltpu.make_async_copy(source, target, in_sems.at[i]))
    for load in inputs[:2] + [load_pages] + inputs[2:]:
        load.start()

    def other(axis, by, flip):
        return device_at(shifted(place, axis, by), lax.rem(core + flip, 2))

    barrier = pltpu.get_barrier_semaphore()
    neighbours = [other(0, 0, 1)] + [
        other(axis, by, flip) for axis in range(3) for by in (1, 2, 3) for flip in (0, 1)
    ]
    for neighbour in neighbours:
        pl.semaphore_signal(barrier, inc=1, device_id=neighbour, device_id_type=MESH_ID)
    pl.semaphore_wait(barrier, len(neighbours))

    def send(source, target, send_sem, recv_sem, device):
        copy = pltpu.make_async_remote_copy(
            src_ref=source, dst_ref=target, send_sem=send_sem, recv_sem=recv_sem,
            device_id=device, device_id_type=MESH_ID,
        )
        copy.start()

    def settle(region, sem):
        pltpu.make_async_copy(region, region, sem).wait()

    def columns(start, count):
        return pl.ds(start * 128, count * 128)

    partner = other(2, 2, 0)
    send(shed_list, wanted_list, shed_sems.at[0], shed_sems.at[1], partner)
    loads = [
        pltpu.make_async_copy(gate_up_hbm, gate_up, w_sems.at[0]),
        pltpu.make_async_copy(down_hbm, down, w_sems.at[1]),
    ]

    for load in inputs[:2]:
        load.wait()
    lane16 = lax.rem(lax.broadcasted_iota(jnp.int32, (16, 128), 1), 16)
    sub16 = lax.broadcasted_iota(jnp.int32, (16, 128), 0)
    repeat = (lane16 == sub16).astype(bf16)
    earlier = (sub16 < lane16).astype(bf16)
    own_ids = ids[...].astype(f32)
    id_rows = jnp.dot(own_ids.astype(bf16), repeat, preferred_element_type=f32)
    gates_left = gate_in[...]
    gate_rows = None
    for _ in range(3):
        piece = gates_left.astype(bf16)
        term = jnp.dot(piece, repeat, preferred_element_type=f32)
        gate_rows = term if gate_rows is None else gate_rows + term
        gates_left = gates_left - piece.astype(f32)
    expert_sub = lax.broadcasted_iota(jnp.int32, (128, 1), 0).astype(f32)
    member = jnp.zeros((128, 16), f32)
    for k in range(8):
        member = jnp.where(own_ids[k : k + 1, :] == expert_sub, 1.0, member)
    before = jnp.dot(member.astype(bf16), earlier, preferred_element_type=f32)
    for k in range(8):
        rank = jnp.sum(
            jnp.where(id_rows[k : k + 1, :] == expert_sub, before, 0.0), axis=0, keepdims=True
        )
        codes[k : k + 1, :] = id_rows[k : k + 1, :] * 2.0 + rank
    codes[8:16, :] = gate_rows
    for i, (axis, by, flip) in enumerate(
        [(0, 0, 1)] + [(a, b, f) for a in range(3) for b in (1, 2, 3) for f in (0, 1)]
    ):
        send(codes, gathered.at[i], code_sems.at[0], code_sems.at[1], other(axis, by, flip))

    load_pages.wait()
    for load in loads:
        load.start()
    settle(wanted_list, shed_sems.at[1])
    to_scalar = pltpu.make_async_copy(wanted_list, wanted_scalar, w_sems.at[3])
    to_scalar.start()
    to_scalar.wait()
    half = shed_out.shape[0] // 2
    for part in range(2):
        for i in range(part * half, part * half + half):
            shed_out[i] = pages[wanted_scalar[0, i]]
        span = pl.ds(part * half, half)
        send(shed_out.at[span], shed_in.at[span], shed_sems.at[2], shed_sems.at[3], partner)

    for load in inputs[2:]:
        load.wait()
    scaling = 1.0 / math.sqrt(HEAD)
    for g in range(GROUPS):
        for h in range(GROUP_HEADS):
            heads[g, h * ROWS : (h + 1) * ROWS, :] = queries[
                :, (g * GROUP_HEADS + h) * HEAD : (g * GROUP_HEADS + h + 1) * HEAD
            ]
    extra[...] = jnp.zeros_like(extra)
    extra[0:ROWS, :] = new_kv[...]
    table = page_table[...].astype(f32)
    diagonal = lax.broadcasted_iota(jnp.int32, (ROWS, ROWS), 0) == lax.broadcasted_iota(
        jnp.int32, (ROWS, ROWS), 1
    )
    length = jnp.sum(
        jnp.where(diagonal, lengths[...].astype(f32), 0.0), axis=1, keepdims=True
    )
    token = lax.broadcasted_iota(jnp.int32, (ROWS, TILE), 1)
    token_page = lax.div(token, PAGE).astype(f32)
    token_place = lax.rem(token, PAGE).astype(f32)

    def allowed(first_page):
        limit = jnp.zeros((ROWS, TILE), f32)
        for j in range(table.shape[1]):
            left = jnp.maximum(length - float(j * PAGE), 0.0)
            limit = limit + jnp.where(table[:, j : j + 1] == token_page + first_page, left, 0.0)
        return token_place < limit

    def masked(values, mask):
        width = values.shape[1]
        values = values.reshape(GROUP_HEADS, ROWS, width)
        return jnp.where(mask[None], values, masked_score).reshape(GROUP_HEADS * ROWS, width)

    def dot_last(left, right):
        return lax.dot_general(
            left, right, (((1,), (1,)), ((), ())), preferred_element_type=f32
        )

    new_mask = lax.broadcasted_iota(jnp.int32, (ROWS, EXTRA), 0) == lax.broadcasted_iota(
        jnp.int32, (ROWS, EXTRA), 1
    )
    for g in range(GROUPS):
        keys = extra[:, g * HEAD : (g + 1) * HEAD]
        values = masked(dot_last(heads[g], keys), new_mask)
        extra_scores[g] = values
        peak[g] = values
    tiles = own_pages // TILE_PAGES

    def score_tile(t, carry):
        mask = allowed((t * TILE_PAGES).astype(f32))
        for g in range(GROUPS):
            keys = pages[pl.ds(t * TILE_PAGES, TILE_PAGES), :, g * HEAD : (g + 1) * HEAD]
            values = masked(dot_last(heads[g], keys.reshape(TILE, HEAD)), mask)
            scores[g, t] = values
            peak[g] = jnp.maximum(peak[g], jnp.maximum(values[:, :128], values[:, 128:]))
        return carry

    lax.fori_loop(0, tiles, score_tile, 0)
    tops = []
    for g in range(GROUPS):
        top = jnp.max(peak[g], axis=1, keepdims=True)
        tops.append(top)
        weights = jnp.exp((extra_scores[g] - top) * scaling)
        weight_sum[g] = weights
        values = extra[:, (GROUPS + g) * HEAD : (GROUPS + g + 1) * HEAD]
        summed[g] = jnp.dot(weights.astype(bf16), values, preferred_element_type=f32)

    def weigh_tile(t, carry):
        for g in range(GROUPS):
            weights = jnp.exp((scores[g, t] - tops[g]) * scaling)
            weight_sum[g] += weights[:, :128] + weights[:, 128:]
            values = pages[
                pl.ds(t * TILE_PAGES, TILE_PAGES), :, (GROUPS + g) * HEAD : (GROUPS + g + 1) * HEAD
            ]
            summed[g] += jnp.dot(
                weights.astype(bf16), values.reshape(TILE, HEAD), preferred_element_type=f32
            )
        return carry

    lax.fori_loop(0, tiles, weigh_tile, 0)
    sums = [jnp.sum(weight_sum[g], axis=1, keepdims=True) for g in range(GROUPS)]

    settle(gathered, code_sems.at[1])

    row = lax.broadcasted_iota(jnp.int32, (256, 1), 0)
    lane = lax.broadcasted_iota(jnp.int32, (1, 128), 1)
    slot = lax.rem(row, 2)
    row_peer = lax.rem(lax.div(row, 2), PEERS)
    same_peer = row_peer == lax.div(lane, 16)
    lane_peer = lax.div(lax.broadcasted_iota(jnp.int32, (16, 128), 1), 16)
    for r, (a0, a1, a2) in enumerate(ROTATIONS):
        entries = jnp.where(lane_peer == 0, codes[...], 0.0)
        entries = jnp.where(lane_peer == 1, gathered[0], entries)
        for s in range(2, PEERS):
            entries = jnp.where(lane_peer == s, gathered[1 + a0 * 6 + s - 2], entries)
        where = list(place)
        where[a1] = lax.rem(place[a1] + lax.div(row, 64), SIDE)
        where[a2] = lax.rem(place[a2] + lax.rem(lax.div(row, 16), SIDE), SIDE)
        x, y, z = where
        expert = lax.div(z, 2) * 64 + x * 16 + lax.rem(z, 2) * 8 + y * 2 + core
        wanted = (expert * 2 + slot).astype(jnp.float32)
        chosen = jnp.zeros((256, 128), jnp.float32)
        gates = jnp.zeros((256, 128), jnp.float32)
        for k in range(8):
            match = same_peer & (entries[k : k + 1, :] == wanted)
            chosen = jnp.where(match, 1.0, chosen)
            gates = jnp.where(match, entries[8 + k : 9 + k, :], gates)
        select[r] = chosen.astype(jnp.bfloat16)
        for part in range(3):
            piece = gates.astype(jnp.bfloat16)
            weight[r, part] = piece
            gates = gates - piece.astype(jnp.float32)


    shed_mask = allowed(float(own_pages))
    settle(shed_in, shed_sems.at[3])
    square = jnp.zeros((ROWS, HEAD), f32)
    for g in range(GROUPS):
        keys = shed_in[:, :, g * HEAD : (g + 1) * HEAD].reshape(TILE, HEAD)
        values = masked(dot_last(heads[g], keys), shed_mask)
        top = jnp.maximum(tops[g], jnp.max(values, axis=1, keepdims=True))
        again = jnp.exp((tops[g] - top) * scaling)
        weights = jnp.exp((values - top) * scaling)
        denominator = sums[g] * again + jnp.sum(weights, axis=1, keepdims=True)
        values = shed_in[:, :, (GROUPS + g) * HEAD : (GROUPS + g + 1) * HEAD].reshape(TILE, HEAD)
        total = summed[g] * again + jnp.dot(
            weights.astype(bf16), values, preferred_element_type=f32
        )
        total = (total / denominator).astype(bf16)
        for h in range(GROUP_HEADS):
            span = pl.ds((g * GROUP_HEADS + h) * HEAD, HEAD)
            part = total[h * ROWS : (h + 1) * ROWS, :]
            attended[:, span] = part
            joined = (residual[:, span].astype(f32) + part.astype(f32)).astype(bf16)
            merged[:, span] = joined
            joined = joined.astype(f32)
            square = square + joined * joined
    write_attended = pltpu.make_async_copy(attended, attended_out, w_sems.at[4])
    write_attended.start()
    width = queries.shape[1]
    mean = jnp.sum(square, axis=1, keepdims=True) * (1.0 / width)
    inverse = lax.rsqrt(mean + epsilon)
    normed[...] = (merged[...].astype(f32) * inverse * gain[...]).astype(bf16)

    for c, (r, start, count) in enumerate(CHUNKS):
        axis = ROTATIONS[r][0]
        for s in range(1, PEERS):
            send(
                normed.at[:, columns(start, count)],
                first.at[s, :, columns(start, count)],
                sent.at[0], s1_r.at[c],
                other(axis, s // 2, s % 2),
            )
    first[0] = normed[...]
    for c, (r, start, count) in enumerate(CHUNKS):
        a1 = ROTATIONS[r][1]
        settle(first.at[pl.ds(1, PEERS - 1), :, columns(start, count)], s1_r.at[c])
        cols = columns(start, count)
        rows = first[:, :, cols].reshape(PEERS * 16, count * 128)
        block = jnp.dot(select[r], rows, preferred_element_type=jnp.float32).astype(jnp.bfloat16)
        block = block.reshape(SIDE, SIDE, 16, count * 128)
        second[0, :, :, cols] = block[0]
        for d in (2, 1, 3):
            packed[d, :, :, cols] = block[d]
        for d in (2, 1, 3):
            send(
                packed.at[d, :, :, cols], second.at[d, :, :, cols],
                sent.at[1], s2_r.at[c], other(a1, d, 0),
            )
    for c, (r, start, count) in enumerate(CHUNKS):
        a2 = ROTATIONS[r][2]
        settle(second.at[pl.ds(1, SIDE - 1), :, :, columns(start, count)], s2_r.at[c])
        cols = columns(start, count)
        for d in (2, 1, 3):
            send(
                second.at[:, d, :, cols], third.at[d, :, :, cols],
                sent.at[2], s3_r.at[c], other(a2, d, 0),
            )
        third[0, :, :, cols] = second[:, 0, :, cols]

    canon = lax.broadcasted_iota(jnp.int32, (256, 256), 0)
    local = lax.broadcasted_iota(jnp.int32, (256, 256), 1)
    apart = (
        lax.rem(lax.div(canon, 4), SIDE),
        lax.rem(lax.div(canon, 16), SIDE),
        lax.div(canon, 64),
    )
    orders = []
    for a0, a1, a2 in ROTATIONS:
        index = apart[a2] * 64 + apart[a1] * 16 + apart[a0] * 4 + lax.rem(canon, 4)
        orders.append((index == local).astype(jnp.bfloat16))

    loads[0].wait()
    for c, (r, start, count) in enumerate(CHUNKS):
        settle(third.at[pl.ds(1, SIDE - 1), :, :, columns(start, count)], s3_r.at[c])
        cols = columns(start, count)
        tokens = third[:, :, :, cols].reshape(256, count * 128)
        if r:
            tokens = jnp.dot(orders[r], tokens, preferred_element_type=jnp.float32)
            tokens = tokens.astype(jnp.bfloat16)
        for n in range(0, 2 * hidden_dim, 512):
            piece = jnp.dot(
                tokens, gate_up[pl.ds(start * 128, count * 128), pl.ds(n, 512)],
                preferred_element_type=jnp.float32,
            )
            if c:
                piece = product[:, pl.ds(n, 512)] + piece
            product[:, pl.ds(n, 512)] = piece
    gate = product[:, :hidden_dim]
    active = (gate / (1.0 + jnp.exp(-gate)) * product[:, hidden_dim:]).astype(jnp.bfloat16)
    hidden[0] = active
    for r in (1, 2):
        turned = lax.dot_general(
            orders[r], active, (((0,), (0,)), ((), ())), preferred_element_type=jnp.float32
        )
        hidden[r] = turned.astype(jnp.bfloat16)

    loads[1].wait()
    for c, (r, start, count) in enumerate(CHUNKS):
        a2 = ROTATIONS[r][2]
        cols = columns(start, count)
        finished = jnp.dot(hidden[r], down[:, cols], preferred_element_type=jnp.float32)
        finished = finished.astype(jnp.bfloat16).reshape(SIDE, SIDE, 16, count * 128)
        back_one[0, :, :, cols] = finished[0]
        for d in (2, 1, 3):
            sent_back[d, :, :, cols] = finished[d]
        for d in (2, 1, 3):
            send(
                sent_back.at[d, :, :, cols], back_one.at[d, :, :, cols],
                sent.at[3], r3_r.at[c], other(a2, -d, 0),
            )
    for c, (r, start, count) in enumerate(CHUNKS):
        a1 = ROTATIONS[r][1]
        settle(back_one.at[pl.ds(1, SIDE - 1), :, :, columns(start, count)], r3_r.at[c])
        cols = columns(start, count)
        for d in (2, 1, 3):
            send(
                back_one.at[:, d, :, cols], back_two.at[d, :, :, cols],
                sent.at[4], r2_r.at[c], other(a1, -d, 0),
            )
        back_two[0, :, :, cols] = back_one[:, 0, :, cols]
    for c, (r, start, count) in enumerate(CHUNKS):
        a0 = ROTATIONS[r][0]
        settle(back_two.at[pl.ds(1, SIDE - 1), :, :, columns(start, count)], r2_r.at[c])
        cols = columns(start, count)
        results = back_two[:, :, :, cols].reshape(256, count * 128)
        total = None
        for part in range(3):
            piece = lax.dot_general(
                weight[r, part], results, (((0,), (0,)), ((), ())),
                preferred_element_type=jnp.float32,
            )
            total = piece if total is None else total + piece
        total = total.reshape(PEERS, 16, count * 128)
        expert_sum[:, cols] = total[0]
        partial[1:, :, cols] = total[1:].astype(jnp.bfloat16)
        for s in range(1, PEERS):
            send(
                partial.at[s, :, cols], back_three.at[s, :, cols],
                sent.at[5], r1_r.at[c], other(a0, -(s // 2), s % 2),
            )
    for c, (r, start, count) in enumerate(CHUNKS):
        settle(back_three.at[pl.ds(1, PEERS - 1), :, columns(start, count)], r1_r.at[c])
        cols = columns(start, count)
        total = expert_sum[:, cols]
        for s in range(1, PEERS):
            total = total + back_three[s, :, cols].astype(jnp.float32)
        merged[:, cols] = (merged[:, cols].astype(jnp.float32) + total).astype(jnp.bfloat16)
    write_layer = pltpu.make_async_copy(merged, layer_out, w_sems.at[5])
    write_layer.start()
    settle(shed_list, shed_sems.at[0])
    settle(gathered, code_sems.at[0])
    settle(shed_out, shed_sems.at[2])
    for i, region in enumerate(
        (
            first.at[pl.ds(1, PEERS - 1)], packed.at[pl.ds(1, SIDE - 1)],
            third.at[pl.ds(1, SIDE - 1)], sent_back.at[pl.ds(1, SIDE - 1)],
            back_two.at[pl.ds(1, SIDE - 1)], partial.at[pl.ds(1, PEERS - 1)],
        )
    ):
        settle(region, sent.at[i])
    write_attended.wait()
    write_layer.wait()


def local(
    queries, new_kv, kv_pages, page_table, lengths, shed_slots, residual, norm_gain,
    expert_ids, gate_weights, w_gate_up, w_down,
):
    rows, width = queries.shape
    gate_up, down = w_gate_up[0], w_down[0]
    hidden_dim = down.shape[0]
    pages, page, kv_width = kv_pages.shape
    shed = shed_slots.shape[0]
    chunks = len(CHUNKS)
    bf16, f32 = jnp.bfloat16, jnp.float32
    hbm = pl.BlockSpec(memory_space=pl.ANY)
    block = pltpu.VMEM((SIDE, SIDE, 16, width), bf16)
    peers = pltpu.VMEM((PEERS, 16, width), bf16)
    dma = pltpu.SemaphoreType.DMA
    group_rows = GROUP_HEADS * ROWS
    attended, layer_out = pl.pallas_call(
        layer_kernel,
        out_shape=(
            jax.ShapeDtypeStruct((rows, width), bf16),
            jax.ShapeDtypeStruct((rows, width), bf16),
        ),
        in_specs=[hbm] * 12,
        out_specs=(hbm, hbm),
        scratch_shapes=[
            pltpu.VMEM((rows, width), bf16),
            pltpu.VMEM((rows, kv_width), bf16),
            pltpu.VMEM(page_table.shape, jnp.int32),
            pltpu.VMEM((1, rows), jnp.int32),
            pltpu.VMEM((rows, width), bf16),
            pltpu.VMEM((1, width), f32),
            pltpu.VMEM((8, rows), jnp.int32),
            pltpu.VMEM((8, rows), f32),
            pltpu.VMEM((rows, width), bf16),
            pltpu.VMEM((rows, width), bf16),
            pltpu.VMEM((rows, width), f32),
            pltpu.VMEM((pages, page, kv_width), bf16),
            pltpu.VMEM((EXTRA, kv_width), bf16),
            pltpu.VMEM((1, shed), jnp.int32),
            pltpu.SMEM((1, shed), jnp.int32),
            pltpu.VMEM((shed, page, kv_width), bf16),
            pltpu.VMEM((shed, page, kv_width), bf16),
            pltpu.VMEM((GROUPS, group_rows, HEAD), bf16),
            pltpu.VMEM((GROUPS, pages // TILE_PAGES, group_rows, TILE), f32),
            pltpu.VMEM((GROUPS, group_rows, EXTRA), f32),
            pltpu.VMEM((GROUPS, group_rows, 128), f32),
            pltpu.VMEM((GROUPS, group_rows, 128), f32),
            pltpu.VMEM((GROUPS, group_rows, HEAD), f32),
            pltpu.VMEM((rows, width), bf16),
            pltpu.VMEM((16, 128), f32),
            pltpu.VMEM(gate_up.shape, bf16),
            pltpu.VMEM(down.shape, bf16),
            pltpu.VMEM((19, 16, 128), f32),
            pltpu.VMEM((3, 256, 128), bf16),
            pltpu.VMEM((3, 3, 256, 128), bf16),
            peers,
            block,
            block,
            block,
            pltpu.VMEM((256, 2 * hidden_dim), f32),
            pltpu.VMEM((3, 256, hidden_dim), bf16),
            block,
            block,
            block,
            peers,
            peers,
            dma((6,)), dma((8,)), dma((4,)), dma((2,)), dma((6,)),
            dma((chunks,)), dma((chunks,)), dma((chunks,)),
            dma((chunks,)), dma((chunks,)), dma((chunks,)),
        ],
        compiler_params=pltpu.CompilerParams(
            collective_id=0, has_side_effects=True, vmem_limit_bytes=52 * 1024 * 1024
        ),
    )(
        *(
            pltpu.with_memory_space_constraint(value, pltpu.HBM)
            for value in (
                queries, new_kv, kv_pages, page_table, lengths.reshape(1, rows),
                shed_slots.reshape(1, shed), residual, norm_gain.reshape(1, width),
                expert_ids.T, gate_weights.T, gate_up, down,
            )
        )
    )
    return (attended, layer_out)


def solution(mesh):
    return jax.shard_map(
        local,
        mesh=mesh,
        in_specs=(
            P(("pool", "dev"), None),
            P(("pool", "dev"), None),
            P(("pool", "dev"), None, None),
            P(("pool", "dev"), None),
            P(("pool", "dev")),
            P(("pool", "dev")),
            P(("pool", "dev"), None),
            P(),
            P(("pool", "dev"), None),
            P(("pool", "dev"), None),
            P(("pool", "dev"), None, None),
            P(("pool", "dev"), None, None),
        ),
        out_specs=(P(("pool", "dev"), None), P(("pool", "dev"), None)),
        check_vma=False,
    )
```

```python
import math

import jax
import jax.numpy as jnp
from jax import lax
from jax.experimental import pallas as pl
from jax.experimental.pallas import tpu as pltpu
from jax.sharding import PartitionSpec as P

HEAD = 128
GROUPS = 2
GROUP_HEADS = 16
ROWS = 16
PAGE = 16
TILE_PAGES = 16
TILE = TILE_PAGES * PAGE
EXTRA = 128

masked_score = -1e30
epsilon = 1e-06

MESH_ID = pl.DeviceIdType.MESH
AHEAD = 3
BEHIND = 1
EARLY = 6
LATE = 3
ROTATIONS = ((0, 1, 2), (1, 2, 0), (2, 0, 1))
SIDE = 4
PEERS = 8
CHUNKS = (
    (0, 0, 4), (1, 4, 4), (2, 8, 4),
    (0, 12, 4), (1, 16, 4), (2, 20, 4),
    (0, 24, 3), (1, 27, 3), (2, 30, 2),
)


def coordinates():
    pool = lax.axis_index("pool")
    dev = lax.axis_index("dev")
    x = lax.div(dev, 16)
    y = lax.rem(lax.div(dev, 2), 4)
    z = pool * 2 + lax.rem(lax.div(dev, 8), 2)
    return (x, y, z), lax.rem(dev, 2)


def device_at(place, core):
    x, y, z = place
    return (lax.div(z, 2), x * 16 + lax.rem(z, 2) * 8 + y * 2 + core)


def shifted(place, axis, by):
    return tuple(
        lax.rem(value + by + SIDE, SIDE) if i == axis else value for i, value in enumerate(place)
    )


def layer_kernel(
    queries_hbm, new_kv_hbm, pages_hbm, page_table_hbm, lengths_hbm, shed_list, residual_hbm,
    gain_hbm, ids_hbm, gate_in_hbm, gate_up_hbm, down_hbm, attended_out, layer_out,
    queries, new_kv, page_table, lengths, residual, gain, ids, gate_in,
    attended, merged, expert_sum,
    pages, extra, wanted_list, wanted_scalar, shed_out, shed_in, heads, scores, extra_scores,
    peak, weight_sum, summed, normed, codes,
    gate_up, down, gathered, select, weight, first, packed, second, third, tokens, product, hidden,
    sent_back, back_one, back_two, partial, near_sum, from_core, back_three,
    w_sems, in_sems, shed_sems, code_sems, sent, core_sems, s1_r, s2_r, s3_r,
    r3_r, r2_r, r1_r, forward_r, core_r,
):
    bf16, f32 = jnp.bfloat16, jnp.float32
    place, core = coordinates()
    hidden_dim = down.shape[0]
    own_pages = pages_hbm.shape[0]
    load_pages = pltpu.make_async_copy(pages_hbm, pages, w_sems.at[2])
    inputs = []
    for i, (source, target) in enumerate(
        (
            (ids_hbm, ids), (gate_in_hbm, gate_in), (page_table_hbm, page_table),
            (lengths_hbm, lengths), (queries_hbm, queries), (new_kv_hbm, new_kv),
            (residual_hbm, residual), (gain_hbm, gain),
        )
    ):
        inputs.append(pltpu.make_async_copy(source, target, in_sems.at[i]))
    for load in inputs[:2] + [load_pages] + inputs[2:]:
        load.start()

    def other(axis, by, flip):
        return device_at(shifted(place, axis, by), lax.rem(core + flip, 2))

    barrier = pltpu.get_barrier_semaphore()
    neighbours = [other(0, 0, 1)] + [
        other(axis, by, flip) for axis in range(3) for by in (1, 2, 3) for flip in (0, 1)
    ]
    for neighbour in neighbours:
        pl.semaphore_signal(barrier, inc=1, device_id=neighbour, device_id_type=MESH_ID)
    pl.semaphore_wait(barrier, len(neighbours))

    def send(source, target, send_sem, recv_sem, device):
        copy = pltpu.make_async_remote_copy(
            src_ref=source, dst_ref=target, send_sem=send_sem, recv_sem=recv_sem,
            device_id=device, device_id_type=MESH_ID,
        )
        copy.start()

    def settle(region, sem):
        pltpu.make_async_copy(region, region, sem).wait()

    def columns(start, count):
        return pl.ds(start * 128, count * 128)

    partner = other(2, 2, 0)
    send(shed_list, wanted_list, shed_sems.at[0], shed_sems.at[1], partner)
    loads = [
        pltpu.make_async_copy(gate_up_hbm, gate_up, w_sems.at[0]),
        pltpu.make_async_copy(down_hbm, down, w_sems.at[1]),
    ]

    for load in inputs[:2]:
        load.wait()
    lane16 = lax.rem(lax.broadcasted_iota(jnp.int32, (16, 128), 1), 16)
    sub16 = lax.broadcasted_iota(jnp.int32, (16, 128), 0)
    repeat = (lane16 == sub16).astype(bf16)
    earlier = (sub16 < lane16).astype(bf16)
    own_ids = ids[...].astype(f32)
    id_rows = jnp.dot(own_ids.astype(bf16), repeat, preferred_element_type=f32)
    gates_left = gate_in[...]
    gate_rows = None
    for _ in range(3):
        piece = gates_left.astype(bf16)
        term = jnp.dot(piece, repeat, preferred_element_type=f32)
        gate_rows = term if gate_rows is None else gate_rows + term
        gates_left = gates_left - piece.astype(f32)
    expert_sub = lax.broadcasted_iota(jnp.int32, (128, 1), 0).astype(f32)
    member = jnp.zeros((128, 16), f32)
    for k in range(8):
        member = jnp.where(own_ids[k : k + 1, :] == expert_sub, 1.0, member)
    before = jnp.dot(member.astype(bf16), earlier, preferred_element_type=f32)
    for k in range(8):
        rank = jnp.sum(
            jnp.where(id_rows[k : k + 1, :] == expert_sub, before, 0.0), axis=0, keepdims=True
        )
        codes[k : k + 1, :] = id_rows[k : k + 1, :] * 2.0 + rank
    codes[8:16, :] = gate_rows
    for i, (axis, by, flip) in enumerate(
        [(0, 0, 1)] + [(a, b, f) for a in range(3) for b in (1, 2, 3) for f in (0, 1)]
    ):
        send(codes, gathered.at[i], code_sems.at[0], code_sems.at[1], other(axis, by, flip))

    load_pages.wait()
    for load in loads:
        load.start()
    settle(wanted_list, shed_sems.at[1])
    to_scalar = pltpu.make_async_copy(wanted_list, wanted_scalar, w_sems.at[3])
    to_scalar.start()
    to_scalar.wait()
    half = shed_out.shape[0] // 2
    for part in range(2):
        for i in range(part * half, part * half + half):
            shed_out[i] = pages[wanted_scalar[0, i]]
        span = pl.ds(part * half, half)
        send(shed_out.at[span], shed_in.at[span], shed_sems.at[2], shed_sems.at[3], partner)

    for load in inputs[2:]:
        load.wait()
    scaling = 1.0 / math.sqrt(HEAD)
    for g in range(GROUPS):
        for h in range(GROUP_HEADS):
            heads[g, h * ROWS : (h + 1) * ROWS, :] = queries[
                :, (g * GROUP_HEADS + h) * HEAD : (g * GROUP_HEADS + h + 1) * HEAD
            ]
    extra[...] = jnp.zeros_like(extra)
    extra[0:ROWS, :] = new_kv[...]
    table = page_table[...].astype(f32)
    diagonal = lax.broadcasted_iota(jnp.int32, (ROWS, ROWS), 0) == lax.broadcasted_iota(
        jnp.int32, (ROWS, ROWS), 1
    )
    length = jnp.sum(
        jnp.where(diagonal, lengths[...].astype(f32), 0.0), axis=1, keepdims=True
    )
    token = lax.broadcasted_iota(jnp.int32, (ROWS, TILE), 1)
    token_page = lax.div(token, PAGE).astype(f32)
    token_place = lax.rem(token, PAGE).astype(f32)

    def allowed(first_page):
        limit = jnp.zeros((ROWS, TILE), f32)
        for j in range(table.shape[1]):
            left = jnp.maximum(length - float(j * PAGE), 0.0)
            limit = limit + jnp.where(table[:, j : j + 1] == token_page + first_page, left, 0.0)
        return token_place < limit

    def masked(values, mask):
        width = values.shape[1]
        values = values.reshape(GROUP_HEADS, ROWS, width)
        return jnp.where(mask[None], values, masked_score).reshape(GROUP_HEADS * ROWS, width)

    def dot_last(left, right):
        return lax.dot_general(
            left, right, (((1,), (1,)), ((), ())), preferred_element_type=f32
        )

    new_mask = lax.broadcasted_iota(jnp.int32, (ROWS, EXTRA), 0) == lax.broadcasted_iota(
        jnp.int32, (ROWS, EXTRA), 1
    )
    for g in range(GROUPS):
        keys = extra[:, g * HEAD : (g + 1) * HEAD]
        values = masked(dot_last(heads[g], keys), new_mask)
        extra_scores[g] = values
        peak[g] = values
    tiles = own_pages // TILE_PAGES

    def score_tile(t, carry):
        mask = allowed((t * TILE_PAGES).astype(f32))
        for g in range(GROUPS):
            keys = pages[pl.ds(t * TILE_PAGES, TILE_PAGES), :, g * HEAD : (g + 1) * HEAD]
            values = masked(dot_last(heads[g], keys.reshape(TILE, HEAD)), mask)
            scores[g, t] = values
            peak[g] = jnp.maximum(peak[g], jnp.maximum(values[:, :128], values[:, 128:]))
        return carry

    lax.fori_loop(0, tiles, score_tile, 0)
    tops = []
    for g in range(GROUPS):
        top = jnp.max(peak[g], axis=1, keepdims=True)
        tops.append(top)
        weights = jnp.exp((extra_scores[g] - top) * scaling)
        weight_sum[g] = weights
        values = extra[:, (GROUPS + g) * HEAD : (GROUPS + g + 1) * HEAD]
        summed[g] = jnp.dot(weights.astype(bf16), values, preferred_element_type=f32)

    def weigh_tile(t, carry):
        for g in range(GROUPS):
            weights = jnp.exp((scores[g, t] - tops[g]) * scaling)
            weight_sum[g] += weights[:, :128] + weights[:, 128:]
            values = pages[
                pl.ds(t * TILE_PAGES, TILE_PAGES), :, (GROUPS + g) * HEAD : (GROUPS + g + 1) * HEAD
            ]
            summed[g] += jnp.dot(
                weights.astype(bf16), values.reshape(TILE, HEAD), preferred_element_type=f32
            )
        return carry

    lax.fori_loop(0, tiles, weigh_tile, 0)
    sums = [jnp.sum(weight_sum[g], axis=1, keepdims=True) for g in range(GROUPS)]

    settle(gathered, code_sems.at[1])

    row = lax.broadcasted_iota(jnp.int32, (256, 1), 0)
    lane = lax.broadcasted_iota(jnp.int32, (1, 128), 1)
    slot = lax.rem(row, 2)
    row_peer = lax.rem(lax.div(row, 2), PEERS)
    same_peer = row_peer == lax.div(lane, 16)
    lane_peer = lax.div(lax.broadcasted_iota(jnp.int32, (16, 128), 1), 16)
    for r, (a0, a1, a2) in enumerate(ROTATIONS):
        entries = jnp.where(lane_peer == 0, codes[...], 0.0)
        entries = jnp.where(lane_peer == SIDE, gathered[0], entries)
        for d in range(1, SIDE):
            for flip in (0, 1):
                entries = jnp.where(
                    lane_peer == flip * SIDE + d, gathered[a0 * 6 + d * 2 - 1 + flip], entries
                )
        where = list(place)
        where[a1] = lax.rem(place[a1] + lax.div(row, 64), SIDE)
        where[a2] = lax.rem(place[a2] + lax.rem(lax.div(row, 16), SIDE), SIDE)
        x, y, z = where
        expert = lax.div(z, 2) * 64 + x * 16 + lax.rem(z, 2) * 8 + y * 2 + core
        wanted = (expert * 2 + slot).astype(jnp.float32)
        chosen = jnp.zeros((256, 128), jnp.float32)
        gates = jnp.zeros((256, 128), jnp.float32)
        for k in range(8):
            match = same_peer & (entries[k : k + 1, :] == wanted)
            chosen = jnp.where(match, 1.0, chosen)
            gates = jnp.where(match, entries[8 + k : 9 + k, :], gates)
        select[r] = chosen.astype(jnp.bfloat16)
        gates = gates.T
        for part in range(3):
            piece = gates.astype(jnp.bfloat16)
            weight[r, part * 128 : (part + 1) * 128, :] = piece
            gates = gates - piece.astype(jnp.float32)


    shed_mask = allowed(float(own_pages))
    settle(shed_in, shed_sems.at[3])
    square = jnp.zeros((ROWS, HEAD), f32)
    for g in range(GROUPS):
        keys = shed_in[:, :, g * HEAD : (g + 1) * HEAD].reshape(TILE, HEAD)
        values = masked(dot_last(heads[g], keys), shed_mask)
        top = jnp.maximum(tops[g], jnp.max(values, axis=1, keepdims=True))
        again = jnp.exp((tops[g] - top) * scaling)
        weights = jnp.exp((values - top) * scaling)
        denominator = sums[g] * again + jnp.sum(weights, axis=1, keepdims=True)
        values = shed_in[:, :, (GROUPS + g) * HEAD : (GROUPS + g + 1) * HEAD].reshape(TILE, HEAD)
        total = summed[g] * again + jnp.dot(
            weights.astype(bf16), values, preferred_element_type=f32
        )
        total = (total / denominator).astype(bf16)
        for h in range(GROUP_HEADS):
            span = pl.ds((g * GROUP_HEADS + h) * HEAD, HEAD)
            part = total[h * ROWS : (h + 1) * ROWS, :]
            attended[:, span] = part
            joined = (residual[:, span].astype(f32) + part.astype(f32)).astype(bf16)
            merged[:, span] = joined
            joined = joined.astype(f32)
            square = square + joined * joined
    write_attended = pltpu.make_async_copy(attended, attended_out, w_sems.at[4])
    write_attended.start()
    width = queries.shape[1]
    mean = jnp.sum(square, axis=1, keepdims=True) * (1.0 / width)
    inverse = lax.rsqrt(mean + epsilon)
    normed[...] = (merged[...].astype(f32) * inverse * gain[...]).astype(bf16)

    sibling = other(0, 0, 1)
    send(normed, first.at[SIDE], core_sems.at[0], core_sems.at[1], sibling)
    for c, (r, start, count) in enumerate(CHUNKS):
        cols = columns(start, count)
        for d in (2, 1, 3):
            send(
                normed.at[:, cols], first.at[d, :, cols],
                sent.at[0], s1_r.at[c], other(ROTATIONS[r][0], d, 0),
            )
            if c < EARLY:
                send(
                    normed.at[:, cols], first.at[SIDE + d, :, cols],
                    core_sems.at[4], forward_r.at[c], other(ROTATIONS[r][0], d, 1),
                )
    first[0] = normed[...]

    def forward(c):
        cols = columns(*CHUNKS[c][1:])
        near = first.at[pl.ds(1, SIDE - 1), :, cols]
        settle(near, s1_r.at[c])
        if c < EARLY:
            return
        send(
            near, first.at[pl.ds(SIDE + 1, SIDE - 1), :, cols],
            core_sems.at[2], forward_r.at[c], sibling,
        )

    settle(first.at[SIDE], core_sems.at[1])
    for c, (r, start, count) in enumerate(CHUNKS):
        a1 = ROTATIONS[r][1]
        if c < EARLY:
            forward(c)
        if EARLY <= c + AHEAD < len(CHUNKS):
            forward(c + AHEAD)
        settle(first.at[pl.ds(SIDE + 1, SIDE - 1), :, columns(start, count)], forward_r.at[c])
        cols = columns(start, count)
        rows = first[:, :, cols].reshape(PEERS * 16, count * 128)
        block = jnp.dot(select[r], rows, preferred_element_type=jnp.float32).astype(jnp.bfloat16)
        block = block.reshape(SIDE, SIDE, 16, count * 128)
        second[0, :, :, cols] = block[0]
        for d in (2, 1, 3):
            packed[d, :, :, cols] = block[d]
        for d in (2, 1, 3):
            send(
                packed.at[d, :, :, cols], second.at[d, :, :, cols],
                sent.at[1], s2_r.at[c], other(a1, d, 0),
            )
    for c, (r, start, count) in enumerate(CHUNKS):
        a2 = ROTATIONS[r][2]
        settle(second.at[pl.ds(1, SIDE - 1), :, :, columns(start, count)], s2_r.at[c])
        cols = columns(start, count)
        for d in (2, 1, 3):
            send(
                second.at[:, d, :, cols], third.at[d, :, :, cols],
                sent.at[2], s3_r.at[c], other(a2, d, 0),
            )
        third[0, :, :, cols] = second[:, 0, :, cols]

    canon = lax.broadcasted_iota(jnp.int32, (256, 256), 0)
    local = lax.broadcasted_iota(jnp.int32, (256, 256), 1)
    apart = (
        lax.rem(lax.div(canon, 2), SIDE),
        lax.rem(lax.div(canon, 16), SIDE),
        lax.div(canon, 64),
    )
    flip = lax.rem(lax.div(canon, 8), 2) * 8
    orders = []
    for a0, a1, a2 in ROTATIONS:
        index = apart[a2] * 64 + apart[a1] * 16 + apart[a0] * 2 + lax.rem(canon, 2) + flip
        orders.append((index == local).astype(jnp.bfloat16))

    loads[0].wait()
    for c, (r, start, count) in enumerate(CHUNKS):
        cols = columns(start, count)
        settle(third.at[pl.ds(1, SIDE - 1), :, :, cols], s3_r.at[c])
        rows = third[:, :, :, cols].reshape(256, count * 128)
        if r:
            rows = jnp.dot(orders[r], rows, preferred_element_type=jnp.float32)
            rows = rows.astype(jnp.bfloat16)
        tokens[:, cols] = rows
        if r < 2:
            continue
        begin = CHUNKS[c - 2][1]
        span = columns(begin, start + count - begin)
        for n in range(0, 2 * hidden_dim, 512):
            piece = jnp.dot(
                tokens[:, span], gate_up[span, pl.ds(n, 512)],
                preferred_element_type=jnp.float32,
            )
            if c > 2:
                piece = product[:, pl.ds(n, 512)] + piece
            product[:, pl.ds(n, 512)] = piece
    gate = product[:, :hidden_dim]
    active = (gate / (1.0 + jnp.exp(-gate)) * product[:, hidden_dim:]).astype(jnp.bfloat16)
    hidden[0] = active
    for r in (1, 2):
        turned = lax.dot_general(
            orders[r], active, (((0,), (0,)), ((), ())), preferred_element_type=jnp.float32
        )
        hidden[r] = turned.astype(jnp.bfloat16)

    loads[1].wait()
    for c, (r, start, count) in enumerate(CHUNKS):
        a2 = ROTATIONS[r][2]
        cols = columns(start, count)
        finished = jnp.dot(hidden[r], down[:, cols], preferred_element_type=jnp.float32)
        finished = finished.astype(jnp.bfloat16).reshape(SIDE, SIDE, 16, count * 128)
        back_one[0, :, :, cols] = finished[0]
        for d in (2, 1, 3):
            sent_back[d, :, :, cols] = finished[d]
        for d in (2, 1, 3):
            send(
                sent_back.at[d, :, :, cols], back_one.at[d, :, :, cols],
                sent.at[3], r3_r.at[c], other(a2, -d, 0),
            )
    for c, (r, start, count) in enumerate(CHUNKS):
        a1 = ROTATIONS[r][1]
        settle(back_one.at[pl.ds(1, SIDE - 1), :, :, columns(start, count)], r3_r.at[c])
        cols = columns(start, count)
        for d in (2, 1, 3):
            send(
                back_one.at[:, d, :, cols], back_two.at[d, :, :, cols],
                sent.at[4], r2_r.at[c], other(a1, -d, 0),
            )
        back_two[0, :, :, cols] = back_one[:, 0, :, cols]
    def combine(c):
        r, start, count = CHUNKS[c]
        cols = columns(start, count)
        settle(back_two.at[pl.ds(1, SIDE - 1), :, :, cols], r2_r.at[c])
        results = back_two[:, :, :, cols].reshape(256, count * 128)
        parts = jnp.dot(weight[r], results, preferred_element_type=jnp.float32)
        total = parts[:128] + parts[128:256] + parts[256:]
        total = total.reshape(2, SIDE, 16, count * 128)
        if c >= LATE:
            expert_sum[:, cols] = total[0, 0]
            partial[0, :, :, cols] = total[1].astype(jnp.bfloat16)
            partial[1, 1:, :, cols] = total[0, 1:].astype(jnp.bfloat16)
            for d in (2, 1, 3):
                send(
                    partial.at[1, d, :, cols], back_three.at[d, :, cols],
                    sent.at[5], r1_r.at[c], other(ROTATIONS[r][0], -d, 0),
                )
                send(
                    partial.at[0, d, :, cols], from_core.at[d, :, cols],
                    core_sems.at[5], core_r.at[c], other(ROTATIONS[r][0], -d, 1),
                )
            send(
                partial.at[0, 0, :, cols], from_core.at[0, :, cols],
                core_sems.at[6], core_r.at[c], sibling,
            )
            return
        near_sum[:, :, cols] = total[0]
        partial[0, :, :, cols] = total[1].astype(jnp.bfloat16)
        send(
            partial.at[0, :, :, cols], from_core.at[:, :, cols],
            core_sems.at[3], core_r.at[c], sibling,
        )

    def pass_on(c):
        r, start, count = CHUNKS[c]
        cols = columns(start, count)
        settle(from_core.at[:, :, cols], core_r.at[c])
        total = near_sum[:, :, cols] + from_core[:, :, cols].astype(jnp.float32)
        expert_sum[:, cols] = total[0]
        partial[1, 1:, :, cols] = total[1:].astype(jnp.bfloat16)
        for d in (2, 1, 3):
            send(
                partial.at[1, d, :, cols], back_three.at[d, :, cols],
                sent.at[5], r1_r.at[c], other(ROTATIONS[r][0], -d, 0),
            )

    for step in range(len(CHUNKS)):
        combine(step)
        if 0 <= step - BEHIND < LATE:
            pass_on(step - BEHIND)
    for c, (r, start, count) in enumerate(CHUNKS):
        cols = columns(start, count)
        settle(back_three.at[pl.ds(1, SIDE - 1), :, cols], r1_r.at[c])
        total = expert_sum[:, cols]
        for d in range(1, SIDE):
            total = total + back_three[d, :, cols].astype(jnp.float32)
        if c >= LATE:
            settle(from_core.at[:, :, cols], core_r.at[c])
            for d in range(SIDE):
                total = total + from_core[d, :, cols].astype(jnp.float32)
        merged[:, cols] = (merged[:, cols].astype(jnp.float32) + total).astype(jnp.bfloat16)
        pltpu.make_async_copy(merged.at[:, cols], layer_out.at[:, cols], w_sems.at[5]).start()
    settle(shed_list, shed_sems.at[0])
    settle(gathered, code_sems.at[0])
    settle(shed_out, shed_sems.at[2])
    settle(normed, core_sems.at[0])
    width = normed.shape[1]
    early = CHUNKS[EARLY][1] * 128
    late = CHUNKS[LATE][1] * 128
    far = pl.ds(SIDE + 1, SIDE - 1)
    settle(first.at[far, :, pl.ds(early, width - early)], core_sems.at[2])
    settle(first.at[far, :, pl.ds(0, early)], core_sems.at[4])
    settle(from_core.at[:, :, pl.ds(0, late)], core_sems.at[3])
    settle(from_core.at[pl.ds(1, SIDE - 1), :, pl.ds(late, width - late)], core_sems.at[5])
    settle(from_core.at[0, :, pl.ds(late, width - late)], core_sems.at[6])
    for i, region in enumerate(
        (
            first.at[pl.ds(1, SIDE - 1)], packed.at[pl.ds(1, SIDE - 1)],
            third.at[pl.ds(1, SIDE - 1)], sent_back.at[pl.ds(1, SIDE - 1)],
            back_two.at[pl.ds(1, SIDE - 1)], partial.at[1, pl.ds(1, SIDE - 1)],
        )
    ):
        settle(region, sent.at[i])
    write_attended.wait()
    settle(merged, w_sems.at[5])


def local(
    queries, new_kv, kv_pages, page_table, lengths, shed_slots, residual, norm_gain,
    expert_ids, gate_weights, w_gate_up, w_down,
):
    rows, width = queries.shape
    gate_up, down = w_gate_up[0], w_down[0]
    hidden_dim = down.shape[0]
    pages, page, kv_width = kv_pages.shape
    shed = shed_slots.shape[0]
    chunks = len(CHUNKS)
    bf16, f32 = jnp.bfloat16, jnp.float32
    hbm = pl.BlockSpec(memory_space=pl.ANY)
    block = pltpu.VMEM((SIDE, SIDE, 16, width), bf16)
    peers = pltpu.VMEM((PEERS, 16, width), bf16)
    dma = pltpu.SemaphoreType.DMA
    group_rows = GROUP_HEADS * ROWS
    attended, layer_out = pl.pallas_call(
        layer_kernel,
        out_shape=(
            jax.ShapeDtypeStruct((rows, width), bf16),
            jax.ShapeDtypeStruct((rows, width), bf16),
        ),
        in_specs=[hbm] * 12,
        out_specs=(hbm, hbm),
        scratch_shapes=[
            pltpu.VMEM((rows, width), bf16),
            pltpu.VMEM((rows, kv_width), bf16),
            pltpu.VMEM(page_table.shape, jnp.int32),
            pltpu.VMEM((1, rows), jnp.int32),
            pltpu.VMEM((rows, width), bf16),
            pltpu.VMEM((1, width), f32),
            pltpu.VMEM((8, rows), jnp.int32),
            pltpu.VMEM((8, rows), f32),
            pltpu.VMEM((rows, width), bf16),
            pltpu.VMEM((rows, width), bf16),
            pltpu.VMEM((rows, width), f32),
            pltpu.VMEM((pages, page, kv_width), bf16),
            pltpu.VMEM((EXTRA, kv_width), bf16),
            pltpu.VMEM((1, shed), jnp.int32),
            pltpu.SMEM((1, shed), jnp.int32),
            pltpu.VMEM((shed, page, kv_width), bf16),
            pltpu.VMEM((shed, page, kv_width), bf16),
            pltpu.VMEM((GROUPS, group_rows, HEAD), bf16),
            pltpu.VMEM((GROUPS, pages // TILE_PAGES, group_rows, TILE), f32),
            pltpu.VMEM((GROUPS, group_rows, EXTRA), f32),
            pltpu.VMEM((GROUPS, group_rows, 128), f32),
            pltpu.VMEM((GROUPS, group_rows, 128), f32),
            pltpu.VMEM((GROUPS, group_rows, HEAD), f32),
            pltpu.VMEM((rows, width), bf16),
            pltpu.VMEM((16, 128), f32),
            pltpu.VMEM(gate_up.shape, bf16),
            pltpu.VMEM(down.shape, bf16),
            pltpu.VMEM((19, 16, 128), f32),
            pltpu.VMEM((3, 256, 128), bf16),
            pltpu.VMEM((3, 3 * 128, 256), bf16),
            peers,
            block,
            block,
            block,
            pltpu.VMEM((256, width), bf16),
            pltpu.VMEM((256, 2 * hidden_dim), f32),
            pltpu.VMEM((3, 256, hidden_dim), bf16),
            block,
            block,
            block,
            pltpu.VMEM((2, SIDE, 16, width), bf16),
            pltpu.VMEM((SIDE, 16, width), f32),
            pltpu.VMEM((SIDE, 16, width), bf16),
            pltpu.VMEM((SIDE, 16, width), bf16),
            dma((6,)), dma((8,)), dma((4,)), dma((2,)), dma((6,)), dma((7,)),
            dma((chunks,)), dma((chunks,)), dma((chunks,)),
            dma((chunks,)), dma((chunks,)), dma((chunks,)),
            dma((chunks,)), dma((chunks,)),
        ],
        compiler_params=pltpu.CompilerParams(
            collective_id=0, has_side_effects=True, vmem_limit_bytes=52 * 1024 * 1024
        ),
    )(
        *(
            pltpu.with_memory_space_constraint(value, pltpu.HBM)
            for value in (
                queries, new_kv, kv_pages, page_table, lengths.reshape(1, rows),
                shed_slots.reshape(1, shed), residual, norm_gain.reshape(1, width),
                expert_ids.T, gate_weights.T, gate_up, down,
            )
        )
    )
    return (attended, layer_out)


def solution(mesh):
    return jax.shard_map(
        local,
        mesh=mesh,
        in_specs=(
            P(("pool", "dev"), None),
            P(("pool", "dev"), None),
            P(("pool", "dev"), None, None),
            P(("pool", "dev"), None),
            P(("pool", "dev")),
            P(("pool", "dev")),
            P(("pool", "dev"), None),
            P(),
            P(("pool", "dev"), None),
            P(("pool", "dev"), None),
            P(("pool", "dev"), None, None),
            P(("pool", "dev"), None, None),
        ),
        out_specs=(P(("pool", "dev"), None), P(("pool", "dev"), None)),
        check_vma=False,
    )
```

```python
import math

import jax
import jax.numpy as jnp
from jax import lax
from jax.experimental import pallas as pl
from jax.experimental.pallas import tpu as pltpu
from jax.sharding import PartitionSpec as P

HEAD = 128
GROUPS = 2
GROUP_HEADS = 16
ROWS = 16
PAGE = 16
TILE_PAGES = 16
TILE = TILE_PAGES * PAGE
EXTRA = 128

masked_score = -1e30
epsilon = 1e-06

MESH_ID = pl.DeviceIdType.MESH
AHEAD = 3
BEHIND = 1
EARLY = 6
LATE = 3
ROTATIONS = ((0, 1, 2), (1, 2, 0), (2, 0, 1))
SIDE = 4
PEERS = 8
CHUNKS = (
    (0, 0, 4), (1, 4, 4), (2, 8, 4),
    (0, 12, 4), (1, 16, 4), (2, 20, 4),
    (0, 24, 3), (1, 27, 3), (2, 30, 2),
)


def coordinates():
    pool = lax.axis_index("pool")
    dev = lax.axis_index("dev")
    x = lax.div(dev, 16)
    y = lax.rem(lax.div(dev, 2), 4)
    z = pool * 2 + lax.rem(lax.div(dev, 8), 2)
    return (x, y, z), lax.rem(dev, 2)


def device_at(place, core):
    x, y, z = place
    return (lax.div(z, 2), x * 16 + lax.rem(z, 2) * 8 + y * 2 + core)


def shifted(place, axis, by):
    return tuple(
        lax.rem(value + by + SIDE, SIDE) if i == axis else value for i, value in enumerate(place)
    )


def layer_kernel(
    queries_hbm, new_kv_hbm, pages_hbm, page_table_hbm, lengths_hbm, shed_list, residual_hbm,
    gain_hbm, ids_hbm, gate_in_hbm, gate_up_hbm, down_hbm, attended_out, layer_out,
    queries, new_kv, page_table, lengths, residual, gain, ids, gate_in,
    attended, merged, expert_sum,
    pages, extra, wanted_list, wanted_scalar, shed_out, shed_in, heads, scores, extra_scores,
    peak, weight_sum, summed, normed, codes,
    gate_up, down, gathered, select, weight, first, packed, second, third, tokens, product, hidden,
    sent_back, back_one, back_two, partial, near_sum, from_core, back_three,
    w_sems, in_sems, shed_sems, code_sems, sent, core_sems, s1_r, s2_r, s3_r,
    r3_r, r2_r, r1_r, forward_r, core_r,
):
    bf16, f32 = jnp.bfloat16, jnp.float32
    place, core = coordinates()
    hidden_dim = down.shape[0]
    own_pages = pages_hbm.shape[0]
    load_pages = pltpu.make_async_copy(pages_hbm, pages, w_sems.at[2])
    inputs = []
    for i, (source, target) in enumerate(
        (
            (ids_hbm, ids), (gate_in_hbm, gate_in), (page_table_hbm, page_table),
            (lengths_hbm, lengths), (queries_hbm, queries), (new_kv_hbm, new_kv),
            (residual_hbm, residual), (gain_hbm, gain),
        )
    ):
        inputs.append(pltpu.make_async_copy(source, target, in_sems.at[i]))
    for load in inputs[:2] + [load_pages] + inputs[2:]:
        load.start()

    def other(axis, by, flip):
        return device_at(shifted(place, axis, by), lax.rem(core + flip, 2))

    barrier = pltpu.get_barrier_semaphore()
    neighbours = [other(0, 0, 1)] + [
        other(axis, by, flip) for axis in range(3) for by in (1, 2, 3) for flip in (0, 1)
    ]
    for neighbour in neighbours:
        pl.semaphore_signal(barrier, inc=1, device_id=neighbour, device_id_type=MESH_ID)
    pl.semaphore_wait(barrier, len(neighbours))

    def send(source, target, send_sem, recv_sem, device):
        copy = pltpu.make_async_remote_copy(
            src_ref=source, dst_ref=target, send_sem=send_sem, recv_sem=recv_sem,
            device_id=device, device_id_type=MESH_ID,
        )
        copy.start()

    def settle(region, sem):
        pltpu.make_async_copy(region, region, sem).wait()

    def columns(start, count):
        return pl.ds(start * 128, count * 128)

    partner = other(2, 2, 0)
    send(shed_list, wanted_list, shed_sems.at[0], shed_sems.at[1], partner)
    loads = [
        pltpu.make_async_copy(gate_up_hbm, gate_up, w_sems.at[0]),
        pltpu.make_async_copy(down_hbm, down, w_sems.at[1]),
    ]

    for load in inputs[:2]:
        load.wait()
    lane16 = lax.rem(lax.broadcasted_iota(jnp.int32, (16, 128), 1), 16)
    sub16 = lax.broadcasted_iota(jnp.int32, (16, 128), 0)
    repeat = (lane16 == sub16).astype(bf16)
    earlier = (sub16 < lane16).astype(bf16)
    own_ids = ids[...].astype(f32)
    id_rows = jnp.dot(own_ids.astype(bf16), repeat, preferred_element_type=f32)
    gates_left = gate_in[...]
    gate_rows = None
    for _ in range(3):
        piece = gates_left.astype(bf16)
        term = jnp.dot(piece, repeat, preferred_element_type=f32)
        gate_rows = term if gate_rows is None else gate_rows + term
        gates_left = gates_left - piece.astype(f32)
    expert_sub = lax.broadcasted_iota(jnp.int32, (128, 1), 0).astype(f32)
    member = jnp.zeros((128, 16), f32)
    for k in range(8):
        member = jnp.where(own_ids[k : k + 1, :] == expert_sub, 1.0, member)
    before = jnp.dot(member.astype(bf16), earlier, preferred_element_type=f32)
    for k in range(8):
        rank = jnp.sum(
            jnp.where(id_rows[k : k + 1, :] == expert_sub, before, 0.0), axis=0, keepdims=True
        )
        codes[k : k + 1, :] = id_rows[k : k + 1, :] * 2.0 + rank
    codes[8:16, :] = gate_rows
    for i, (axis, by, flip) in enumerate(
        [(0, 0, 1)] + [(a, b, f) for a in range(3) for b in (1, 2, 3) for f in (0, 1)]
    ):
        send(codes, gathered.at[i], code_sems.at[0], code_sems.at[1], other(axis, by, flip))

    load_pages.wait()
    for load in loads:
        load.start()
    settle(wanted_list, shed_sems.at[1])
    to_scalar = pltpu.make_async_copy(wanted_list, wanted_scalar, w_sems.at[3])
    to_scalar.start()
    to_scalar.wait()
    half = shed_out.shape[2] // 2
    for part in range(2):
        span = pl.ds(part * half, half)
        for i in range(shed_out.shape[0]):
            shed_out[i, :, span] = pages[wanted_scalar[0, i], :, span]
        send(
            shed_out.at[:, :, span], shed_in.at[:, :, span],
            shed_sems.at[2], shed_sems.at[3 + part], partner,
        )

    for load in inputs[2:]:
        load.wait()
    scaling = 1.0 / math.sqrt(HEAD)
    for g in range(GROUPS):
        for h in range(GROUP_HEADS):
            heads[g, h * ROWS : (h + 1) * ROWS, :] = queries[
                :, (g * GROUP_HEADS + h) * HEAD : (g * GROUP_HEADS + h + 1) * HEAD
            ]
    extra[...] = jnp.zeros_like(extra)
    extra[0:ROWS, :] = new_kv[...]
    table = page_table[...].astype(f32)
    diagonal = lax.broadcasted_iota(jnp.int32, (ROWS, ROWS), 0) == lax.broadcasted_iota(
        jnp.int32, (ROWS, ROWS), 1
    )
    length = jnp.sum(
        jnp.where(diagonal, lengths[...].astype(f32), 0.0), axis=1, keepdims=True
    )
    token = lax.broadcasted_iota(jnp.int32, (ROWS, TILE), 1)
    token_page = lax.div(token, PAGE).astype(f32)
    token_place = lax.rem(token, PAGE).astype(f32)

    def allowed(first_page):
        limit = jnp.zeros((ROWS, TILE), f32)
        for j in range(table.shape[1]):
            left = jnp.maximum(length - float(j * PAGE), 0.0)
            limit = limit + jnp.where(table[:, j : j + 1] == token_page + first_page, left, 0.0)
        return token_place < limit

    def masked(values, mask):
        width = values.shape[1]
        values = values.reshape(GROUP_HEADS, ROWS, width)
        return jnp.where(mask[None], values, masked_score).reshape(GROUP_HEADS * ROWS, width)

    def dot_last(left, right):
        return lax.dot_general(
            left, right, (((1,), (1,)), ((), ())), preferred_element_type=f32
        )

    new_mask = lax.broadcasted_iota(jnp.int32, (ROWS, EXTRA), 0) == lax.broadcasted_iota(
        jnp.int32, (ROWS, EXTRA), 1
    )
    for g in range(GROUPS):
        keys = extra[:, g * HEAD : (g + 1) * HEAD]
        values = masked(dot_last(heads[g], keys), new_mask)
        extra_scores[g] = values
        peak[g] = values
    tiles = own_pages // TILE_PAGES

    def score_tile(t, carry):
        mask = allowed((t * TILE_PAGES).astype(f32))
        for g in range(GROUPS):
            keys = pages[pl.ds(t * TILE_PAGES, TILE_PAGES), :, g * HEAD : (g + 1) * HEAD]
            values = masked(dot_last(heads[g], keys.reshape(TILE, HEAD)), mask)
            scores[g, t] = values
            peak[g] = jnp.maximum(peak[g], jnp.maximum(values[:, :128], values[:, 128:]))
        return carry

    lax.fori_loop(0, tiles, score_tile, 0)
    tops = []
    for g in range(GROUPS):
        top = jnp.max(peak[g], axis=1, keepdims=True)
        tops.append(top)
        weights = jnp.exp((extra_scores[g] - top) * scaling)
        weight_sum[g] = weights
        values = extra[:, (GROUPS + g) * HEAD : (GROUPS + g + 1) * HEAD]
        summed[g] = jnp.dot(weights.astype(bf16), values, preferred_element_type=f32)

    def weigh_tile(t, carry):
        for g in range(GROUPS):
            weights = jnp.exp((scores[g, t] - tops[g]) * scaling)
            weight_sum[g] += weights[:, :128] + weights[:, 128:]
            values = pages[
                pl.ds(t * TILE_PAGES, TILE_PAGES), :, (GROUPS + g) * HEAD : (GROUPS + g + 1) * HEAD
            ]
            summed[g] += jnp.dot(
                weights.astype(bf16), values.reshape(TILE, HEAD), preferred_element_type=f32
            )
        return carry

    lax.fori_loop(0, tiles, weigh_tile, 0)
    sums = [jnp.sum(weight_sum[g], axis=1, keepdims=True) for g in range(GROUPS)]

    settle(gathered, code_sems.at[1])

    row = lax.broadcasted_iota(jnp.int32, (256, 1), 0)
    lane = lax.broadcasted_iota(jnp.int32, (1, 128), 1)
    slot = lax.rem(row, 2)
    row_peer = lax.rem(lax.div(row, 2), PEERS)
    same_peer = row_peer == lax.div(lane, 16)
    lane_peer = lax.div(lax.broadcasted_iota(jnp.int32, (16, 128), 1), 16)
    for r, (a0, a1, a2) in enumerate(ROTATIONS):
        entries = jnp.where(lane_peer == 0, codes[...], 0.0)
        entries = jnp.where(lane_peer == SIDE, gathered[0], entries)
        for d in range(1, SIDE):
            for flip in (0, 1):
                entries = jnp.where(
                    lane_peer == flip * SIDE + d, gathered[a0 * 6 + d * 2 - 1 + flip], entries
                )
        where = list(place)
        where[a1] = lax.rem(place[a1] + lax.div(row, 64), SIDE)
        where[a2] = lax.rem(place[a2] + lax.rem(lax.div(row, 16), SIDE), SIDE)
        x, y, z = where
        expert = lax.div(z, 2) * 64 + x * 16 + lax.rem(z, 2) * 8 + y * 2 + core
        wanted = (expert * 2 + slot).astype(jnp.float32)
        chosen = jnp.zeros((256, 128), jnp.float32)
        gates = jnp.zeros((256, 128), jnp.float32)
        for k in range(8):
            match = same_peer & (entries[k : k + 1, :] == wanted)
            chosen = jnp.where(match, 1.0, chosen)
            gates = jnp.where(match, entries[8 + k : 9 + k, :], gates)
        select[r] = chosen.astype(jnp.bfloat16)
        gates = gates.T
        for part in range(3):
            piece = gates.astype(jnp.bfloat16)
            weight[r, part * 128 : (part + 1) * 128, :] = piece
            gates = gates - piece.astype(jnp.float32)


    shed_mask = allowed(float(own_pages))
    settle(shed_in.at[:, :, pl.ds(0, half)], shed_sems.at[3])
    late_parts = []
    for g in range(GROUPS):
        keys = shed_in[:, :, g * HEAD : (g + 1) * HEAD].reshape(TILE, HEAD)
        values = masked(dot_last(heads[g], keys), shed_mask)
        top = jnp.maximum(tops[g], jnp.max(values, axis=1, keepdims=True))
        again = jnp.exp((tops[g] - top) * scaling)
        weights = jnp.exp((values - top) * scaling)
        denominator = sums[g] * again + jnp.sum(weights, axis=1, keepdims=True)
        inverse = 1.0 / denominator
        summed[g] = summed[g] * (again * inverse)
        late_parts.append((weights.astype(bf16), inverse))
    settle(shed_in.at[:, :, pl.ds(half, half)], shed_sems.at[4])
    square = jnp.zeros((ROWS, HEAD), f32)
    for g in range(GROUPS):
        weights, inverse = late_parts[g]
        values = shed_in[:, :, (GROUPS + g) * HEAD : (GROUPS + g + 1) * HEAD].reshape(TILE, HEAD)
        total = summed[g] + jnp.dot(weights, values, preferred_element_type=f32) * inverse
        total = total.astype(bf16)
        for h in range(GROUP_HEADS):
            span = pl.ds((g * GROUP_HEADS + h) * HEAD, HEAD)
            part = total[h * ROWS : (h + 1) * ROWS, :]
            attended[:, span] = part
            joined = (residual[:, span].astype(f32) + part.astype(f32)).astype(bf16)
            merged[:, span] = joined
            joined = joined.astype(f32)
            square = square + joined * joined
    write_attended = pltpu.make_async_copy(attended, attended_out, w_sems.at[4])
    write_attended.start()
    width = queries.shape[1]
    mean = jnp.sum(square, axis=1, keepdims=True) * (1.0 / width)
    inverse = lax.rsqrt(mean + epsilon)
    normed[...] = (merged[...].astype(f32) * inverse * gain[...]).astype(bf16)

    sibling = other(0, 0, 1)
    send(normed, first.at[SIDE], core_sems.at[0], core_sems.at[1], sibling)
    for c, (r, start, count) in enumerate(CHUNKS):
        cols = columns(start, count)
        for d in (2, 1, 3):
            send(
                normed.at[:, cols], first.at[d, :, cols],
                sent.at[0], s1_r.at[c], other(ROTATIONS[r][0], d, 0),
            )
            if c < EARLY:
                send(
                    normed.at[:, cols], first.at[SIDE + d, :, cols],
                    core_sems.at[4], forward_r.at[c], other(ROTATIONS[r][0], d, 1),
                )
    first[0] = normed[...]

    def forward(c):
        cols = columns(*CHUNKS[c][1:])
        near = first.at[pl.ds(1, SIDE - 1), :, cols]
        settle(near, s1_r.at[c])
        if c < EARLY:
            return
        send(
            near, first.at[pl.ds(SIDE + 1, SIDE - 1), :, cols],
            core_sems.at[2], forward_r.at[c], sibling,
        )

    settle(first.at[SIDE], core_sems.at[1])
    for c, (r, start, count) in enumerate(CHUNKS):
        a1 = ROTATIONS[r][1]
        if c < EARLY:
            forward(c)
        if EARLY <= c + AHEAD < len(CHUNKS):
            forward(c + AHEAD)
        settle(first.at[pl.ds(SIDE + 1, SIDE - 1), :, columns(start, count)], forward_r.at[c])
        cols = columns(start, count)
        rows = first[:, :, cols].reshape(PEERS * 16, count * 128)
        block = jnp.dot(select[r], rows, preferred_element_type=jnp.float32).astype(jnp.bfloat16)
        block = block.reshape(SIDE, SIDE, 16, count * 128)
        second[0, :, :, cols] = block[0]
        for d in (2, 1, 3):
            packed[d, :, :, cols] = block[d]
        for d in (2, 1, 3):
            send(
                packed.at[d, :, :, cols], second.at[d, :, :, cols],
                sent.at[1], s2_r.at[c], other(a1, d, 0),
            )
    for c, (r, start, count) in enumerate(CHUNKS):
        a2 = ROTATIONS[r][2]
        settle(second.at[pl.ds(1, SIDE - 1), :, :, columns(start, count)], s2_r.at[c])
        cols = columns(start, count)
        for d in (2, 1, 3):
            send(
                second.at[:, d, :, cols], third.at[d, :, :, cols],
                sent.at[2], s3_r.at[c], other(a2, d, 0),
            )
        third[0, :, :, cols] = second[:, 0, :, cols]

    canon = lax.broadcasted_iota(jnp.int32, (256, 256), 0)
    local = lax.broadcasted_iota(jnp.int32, (256, 256), 1)
    apart = (
        lax.rem(lax.div(canon, 2), SIDE),
        lax.rem(lax.div(canon, 16), SIDE),
        lax.div(canon, 64),
    )
    flip = lax.rem(lax.div(canon, 8), 2) * 8
    orders = []
    for a0, a1, a2 in ROTATIONS:
        index = apart[a2] * 64 + apart[a1] * 16 + apart[a0] * 2 + lax.rem(canon, 2) + flip
        orders.append((index == local).astype(jnp.bfloat16))

    loads[0].wait()
    for c, (r, start, count) in enumerate(CHUNKS):
        cols = columns(start, count)
        settle(third.at[pl.ds(1, SIDE - 1), :, :, cols], s3_r.at[c])
        rows = third[:, :, :, cols].reshape(256, count * 128)
        if r:
            rows = jnp.dot(orders[r], rows, preferred_element_type=jnp.float32)
            rows = rows.astype(jnp.bfloat16)
        tokens[:, cols] = rows
        if r < 2:
            continue
        begin = CHUNKS[c - 2][1]
        span = columns(begin, start + count - begin)
        for n in range(0, 2 * hidden_dim, 512):
            piece = jnp.dot(
                tokens[:, span], gate_up[span, pl.ds(n, 512)],
                preferred_element_type=jnp.float32,
            )
            if c > 2:
                piece = product[:, pl.ds(n, 512)] + piece
            product[:, pl.ds(n, 512)] = piece
    gate = product[:, :hidden_dim]
    active = (gate / (1.0 + jnp.exp(-gate)) * product[:, hidden_dim:]).astype(jnp.bfloat16)
    hidden[0] = active

    loads[1].wait()
    for c, (r, start, count) in enumerate(CHUNKS):
        a2 = ROTATIONS[r][2]
        cols = columns(start, count)
        if c in (1, 2):
            turned = lax.dot_general(
                orders[r], active, (((0,), (0,)), ((), ())), preferred_element_type=jnp.float32
            )
            hidden[r] = turned.astype(jnp.bfloat16)
        finished = jnp.dot(hidden[r], down[:, cols], preferred_element_type=jnp.float32)
        finished = finished.astype(jnp.bfloat16).reshape(SIDE, SIDE, 16, count * 128)
        back_one[0, :, :, cols] = finished[0]
        for d in (2, 1, 3):
            sent_back[d, :, :, cols] = finished[d]
        for d in (2, 1, 3):
            send(
                sent_back.at[d, :, :, cols], back_one.at[d, :, :, cols],
                sent.at[3], r3_r.at[c], other(a2, -d, 0),
            )
    for c, (r, start, count) in enumerate(CHUNKS):
        a1 = ROTATIONS[r][1]
        settle(back_one.at[pl.ds(1, SIDE - 1), :, :, columns(start, count)], r3_r.at[c])
        cols = columns(start, count)
        for d in (2, 1, 3):
            send(
                back_one.at[:, d, :, cols], back_two.at[d, :, :, cols],
                sent.at[4], r2_r.at[c], other(a1, -d, 0),
            )
        back_two[0, :, :, cols] = back_one[:, 0, :, cols]
    def combine(c):
        r, start, count = CHUNKS[c]
        cols = columns(start, count)
        settle(back_two.at[pl.ds(1, SIDE - 1), :, :, cols], r2_r.at[c])
        results = back_two[:, :, :, cols].reshape(256, count * 128)
        parts = jnp.dot(weight[r], results, preferred_element_type=jnp.float32)
        total = parts[:128] + parts[128:256] + parts[256:]
        total = total.reshape(2, SIDE, 16, count * 128)
        if c >= LATE:
            expert_sum[:, cols] = total[0, 0]
            partial[0, :, :, cols] = total[1].astype(jnp.bfloat16)
            partial[1, 1:, :, cols] = total[0, 1:].astype(jnp.bfloat16)
            for d in (2, 1, 3):
                send(
                    partial.at[1, d, :, cols], back_three.at[d, :, cols],
                    sent.at[5], r1_r.at[c], other(ROTATIONS[r][0], -d, 0),
                )
                send(
                    partial.at[0, d, :, cols], from_core.at[d, :, cols],
                    core_sems.at[5], core_r.at[c], other(ROTATIONS[r][0], -d, 1),
                )
            send(
                partial.at[0, 0, :, cols], from_core.at[0, :, cols],
                core_sems.at[6], core_r.at[c], sibling,
            )
            return
        near_sum[:, :, cols] = total[0]
        partial[0, :, :, cols] = total[1].astype(jnp.bfloat16)
        send(
            partial.at[0, :, :, cols], from_core.at[:, :, cols],
            core_sems.at[3], core_r.at[c], sibling,
        )

    def pass_on(c):
        r, start, count = CHUNKS[c]
        cols = columns(start, count)
        settle(from_core.at[:, :, cols], core_r.at[c])
        total = near_sum[:, :, cols] + from_core[:, :, cols].astype(jnp.float32)
        expert_sum[:, cols] = total[0]
        partial[1, 1:, :, cols] = total[1:].astype(jnp.bfloat16)
        for d in (2, 1, 3):
            send(
                partial.at[1, d, :, cols], back_three.at[d, :, cols],
                sent.at[5], r1_r.at[c], other(ROTATIONS[r][0], -d, 0),
            )

    for step in range(len(CHUNKS)):
        combine(step)
        if 0 <= step - BEHIND < LATE:
            pass_on(step - BEHIND)
    for c, (r, start, count) in enumerate(CHUNKS):
        cols = columns(start, count)
        settle(back_three.at[pl.ds(1, SIDE - 1), :, cols], r1_r.at[c])
        total = expert_sum[:, cols]
        for d in range(1, SIDE):
            total = total + back_three[d, :, cols].astype(jnp.float32)
        if c >= LATE:
            settle(from_core.at[:, :, cols], core_r.at[c])
            for d in range(SIDE):
                total = total + from_core[d, :, cols].astype(jnp.float32)
        merged[:, cols] = (merged[:, cols].astype(jnp.float32) + total).astype(jnp.bfloat16)
        pltpu.make_async_copy(merged.at[:, cols], layer_out.at[:, cols], w_sems.at[5]).start()
    settle(shed_list, shed_sems.at[0])
    settle(gathered, code_sems.at[0])
    settle(shed_out, shed_sems.at[2])
    settle(normed, core_sems.at[0])
    width = normed.shape[1]
    early = CHUNKS[EARLY][1] * 128
    late = CHUNKS[LATE][1] * 128
    far = pl.ds(SIDE + 1, SIDE - 1)
    settle(first.at[far, :, pl.ds(early, width - early)], core_sems.at[2])
    settle(first.at[far, :, pl.ds(0, early)], core_sems.at[4])
    settle(from_core.at[:, :, pl.ds(0, late)], core_sems.at[3])
    settle(from_core.at[pl.ds(1, SIDE - 1), :, pl.ds(late, width - late)], core_sems.at[5])
    settle(from_core.at[0, :, pl.ds(late, width - late)], core_sems.at[6])
    for i, region in enumerate(
        (
            first.at[pl.ds(1, SIDE - 1)], packed.at[pl.ds(1, SIDE - 1)],
            third.at[pl.ds(1, SIDE - 1)], sent_back.at[pl.ds(1, SIDE - 1)],
            back_two.at[pl.ds(1, SIDE - 1)], partial.at[1, pl.ds(1, SIDE - 1)],
        )
    ):
        settle(region, sent.at[i])
    write_attended.wait()
    settle(merged, w_sems.at[5])


def local(
    queries, new_kv, kv_pages, page_table, lengths, shed_slots, residual, norm_gain,
    expert_ids, gate_weights, w_gate_up, w_down,
):
    rows, width = queries.shape
    gate_up, down = w_gate_up[0], w_down[0]
    hidden_dim = down.shape[0]
    pages, page, kv_width = kv_pages.shape
    shed = shed_slots.shape[0]
    chunks = len(CHUNKS)
    bf16, f32 = jnp.bfloat16, jnp.float32
    hbm = pl.BlockSpec(memory_space=pl.ANY)
    block = pltpu.VMEM((SIDE, SIDE, 16, width), bf16)
    peers = pltpu.VMEM((PEERS, 16, width), bf16)
    dma = pltpu.SemaphoreType.DMA
    group_rows = GROUP_HEADS * ROWS
    attended, layer_out = pl.pallas_call(
        layer_kernel,
        out_shape=(
            jax.ShapeDtypeStruct((rows, width), bf16),
            jax.ShapeDtypeStruct((rows, width), bf16),
        ),
        in_specs=[hbm] * 12,
        out_specs=(hbm, hbm),
        scratch_shapes=[
            pltpu.VMEM((rows, width), bf16),
            pltpu.VMEM((rows, kv_width), bf16),
            pltpu.VMEM(page_table.shape, jnp.int32),
            pltpu.VMEM((1, rows), jnp.int32),
            pltpu.VMEM((rows, width), bf16),
            pltpu.VMEM((1, width), f32),
            pltpu.VMEM((8, rows), jnp.int32),
            pltpu.VMEM((8, rows), f32),
            pltpu.VMEM((rows, width), bf16),
            pltpu.VMEM((rows, width), bf16),
            pltpu.VMEM((rows, width), f32),
            pltpu.VMEM((pages, page, kv_width), bf16),
            pltpu.VMEM((EXTRA, kv_width), bf16),
            pltpu.VMEM((1, shed), jnp.int32),
            pltpu.SMEM((1, shed), jnp.int32),
            pltpu.VMEM((shed, page, kv_width), bf16),
            pltpu.VMEM((shed, page, kv_width), bf16),
            pltpu.VMEM((GROUPS, group_rows, HEAD), bf16),
            pltpu.VMEM((GROUPS, pages // TILE_PAGES, group_rows, TILE), f32),
            pltpu.VMEM((GROUPS, group_rows, EXTRA), f32),
            pltpu.VMEM((GROUPS, group_rows, 128), f32),
            pltpu.VMEM((GROUPS, group_rows, 128), f32),
            pltpu.VMEM((GROUPS, group_rows, HEAD), f32),
            pltpu.VMEM((rows, width), bf16),
            pltpu.VMEM((16, 128), f32),
            pltpu.VMEM(gate_up.shape, bf16),
            pltpu.VMEM(down.shape, bf16),
            pltpu.VMEM((19, 16, 128), f32),
            pltpu.VMEM((3, 256, 128), bf16),
            pltpu.VMEM((3, 3 * 128, 256), bf16),
            peers,
            block,
            block,
            block,
            pltpu.VMEM((256, width), bf16),
            pltpu.VMEM((256, 2 * hidden_dim), f32),
            pltpu.VMEM((3, 256, hidden_dim), bf16),
            block,
            block,
            block,
            pltpu.VMEM((2, SIDE, 16, width), bf16),
            pltpu.VMEM((SIDE, 16, width), f32),
            pltpu.VMEM((SIDE, 16, width), bf16),
            pltpu.VMEM((SIDE, 16, width), bf16),
            dma((6,)), dma((8,)), dma((5,)), dma((2,)), dma((6,)), dma((7,)),
            dma((chunks,)), dma((chunks,)), dma((chunks,)),
            dma((chunks,)), dma((chunks,)), dma((chunks,)),
            dma((chunks,)), dma((chunks,)),
        ],
        compiler_params=pltpu.CompilerParams(
            collective_id=0, has_side_effects=True, vmem_limit_bytes=52 * 1024 * 1024
        ),
    )(
        *(
            pltpu.with_memory_space_constraint(value, pltpu.HBM)
            for value in (
                queries, new_kv, kv_pages, page_table, lengths.reshape(1, rows),
                shed_slots.reshape(1, shed), residual, norm_gain.reshape(1, width),
                expert_ids.T, gate_weights.T, gate_up, down,
            )
        )
    )
    return (attended, layer_out)


def solution(mesh):
    return jax.shard_map(
        local,
        mesh=mesh,
        in_specs=(
            P(("pool", "dev"), None),
            P(("pool", "dev"), None),
            P(("pool", "dev"), None, None),
            P(("pool", "dev"), None),
            P(("pool", "dev")),
            P(("pool", "dev")),
            P(("pool", "dev"), None),
            P(),
            P(("pool", "dev"), None),
            P(("pool", "dev"), None),
            P(("pool", "dev"), None, None),
            P(("pool", "dev"), None, None),
        ),
        out_specs=(P(("pool", "dev"), None), P(("pool", "dev"), None)),
        check_vma=False,
    )
```

```python
import math

import jax
import jax.numpy as jnp
from jax import lax
from jax.experimental import pallas as pl
from jax.experimental.pallas import tpu as pltpu
from jax.sharding import PartitionSpec as P

HEAD = 128
GROUPS = 2
GROUP_HEADS = 16
ROWS = 16
PAGE = 16
TILE_PAGES = 16
TILE = TILE_PAGES * PAGE
EXTRA = 128

masked_score = -1e30
epsilon = 1e-06

MESH_ID = pl.DeviceIdType.MESH
AHEAD = 3
BEHIND = 1
EARLY = 6
LATE = 3
ROTATIONS = ((0, 1, 2), (1, 2, 0), (2, 0, 1))
SIDE = 4
PEERS = 8
CHUNKS = (
    (0, 0, 4), (1, 4, 4), (2, 8, 4),
    (0, 12, 4), (1, 16, 4), (2, 20, 4),
    (0, 24, 3), (1, 27, 3), (2, 30, 2),
)


def coordinates():
    pool = lax.axis_index("pool")
    dev = lax.axis_index("dev")
    x = lax.div(dev, 16)
    y = lax.rem(lax.div(dev, 2), 4)
    z = pool * 2 + lax.rem(lax.div(dev, 8), 2)
    return (x, y, z), lax.rem(dev, 2)


def device_at(place, core):
    x, y, z = place
    return (lax.div(z, 2), x * 16 + lax.rem(z, 2) * 8 + y * 2 + core)


def shifted(place, axis, by):
    return tuple(
        lax.rem(value + by + SIDE, SIDE) if i == axis else value for i, value in enumerate(place)
    )


def layer_kernel(
    queries_hbm, new_kv_hbm, pages_hbm, page_table_hbm, lengths_hbm, shed_list, residual_hbm,
    gain_hbm, ids_hbm, gate_in_hbm, gate_up_hbm, down_hbm, attended_out, layer_out,
    queries, new_kv, page_table, lengths, residual, gain, ids, gate_in,
    attended, merged, expert_sum,
    pages, extra, wanted_list, wanted_scalar, shed_out, shed_in, heads, scores, extra_scores,
    peak, weight_sum, summed, normed, codes,
    gate_up, down, gathered, select, weight, first, packed, second, third, tokens, product, hidden,
    sent_back, back_one, back_two, partial, near_sum, from_core, back_three,
    w_sems, in_sems, shed_sems, code_sems, sent, core_sems, s1_r, s2_r, s3_r,
    r3_r, r2_r, r1_r, forward_r, core_r,
):
    bf16, f32 = jnp.bfloat16, jnp.float32
    place, core = coordinates()
    hidden_dim = down.shape[0]
    own_pages = pages_hbm.shape[0]
    load_pages = pltpu.make_async_copy(pages_hbm, pages, w_sems.at[2])
    inputs = []
    for i, (source, target) in enumerate(
        (
            (ids_hbm, ids), (gate_in_hbm, gate_in), (page_table_hbm, page_table),
            (lengths_hbm, lengths), (queries_hbm, queries), (new_kv_hbm, new_kv),
            (residual_hbm, residual), (gain_hbm, gain),
        )
    ):
        inputs.append(pltpu.make_async_copy(source, target, in_sems.at[i]))
    for load in inputs[:2] + [load_pages] + inputs[2:]:
        load.start()

    def other(axis, by, flip):
        return device_at(shifted(place, axis, by), lax.rem(core + flip, 2))

    barrier = pltpu.get_barrier_semaphore()
    neighbours = [other(0, 0, 1)] + [
        other(axis, by, flip) for axis in range(3) for by in (1, 2, 3) for flip in (0, 1)
    ]
    for neighbour in neighbours:
        pl.semaphore_signal(barrier, inc=1, device_id=neighbour, device_id_type=MESH_ID)
    pl.semaphore_wait(barrier, len(neighbours))

    def send(source, target, send_sem, recv_sem, device):
        copy = pltpu.make_async_remote_copy(
            src_ref=source, dst_ref=target, send_sem=send_sem, recv_sem=recv_sem,
            device_id=device, device_id_type=MESH_ID,
        )
        copy.start()

    def settle(region, sem):
        pltpu.make_async_copy(region, region, sem).wait()

    def columns(start, count):
        return pl.ds(start * 128, count * 128)

    partner = other(2, 2, 0)
    send(shed_list, wanted_list, shed_sems.at[0], shed_sems.at[1], partner)
    loads = [
        pltpu.make_async_copy(gate_up_hbm, gate_up, w_sems.at[0]),
        pltpu.make_async_copy(down_hbm, down, w_sems.at[1]),
    ]

    for load in inputs[:2]:
        load.wait()
    lane16 = lax.rem(lax.broadcasted_iota(jnp.int32, (16, 128), 1), 16)
    sub16 = lax.broadcasted_iota(jnp.int32, (16, 128), 0)
    repeat = (lane16 == sub16).astype(bf16)
    earlier = (sub16 < lane16).astype(bf16)
    own_ids = ids[...].astype(f32)
    id_rows = jnp.dot(own_ids.astype(bf16), repeat, preferred_element_type=f32)
    gates_left = gate_in[...]
    gate_rows = None
    for _ in range(3):
        piece = gates_left.astype(bf16)
        term = jnp.dot(piece, repeat, preferred_element_type=f32)
        gate_rows = term if gate_rows is None else gate_rows + term
        gates_left = gates_left - piece.astype(f32)
    expert_sub = lax.broadcasted_iota(jnp.int32, (128, 1), 0).astype(f32)
    member = jnp.zeros((128, 16), f32)
    for k in range(8):
        member = jnp.where(own_ids[k : k + 1, :] == expert_sub, 1.0, member)
    before = jnp.dot(member.astype(bf16), earlier, preferred_element_type=f32)
    for k in range(8):
        rank = jnp.sum(
            jnp.where(id_rows[k : k + 1, :] == expert_sub, before, 0.0), axis=0, keepdims=True
        )
        codes[k : k + 1, :] = id_rows[k : k + 1, :] * 2.0 + rank
    codes[8:16, :] = gate_rows
    for i, (axis, by, flip) in enumerate(
        [(0, 0, 1)] + [(a, b, f) for a in range(3) for b in (1, 2, 3) for f in (0, 1)]
    ):
        send(codes, gathered.at[i], code_sems.at[0], code_sems.at[1], other(axis, by, flip))

    load_pages.wait()
    for load in loads:
        load.start()
    settle(wanted_list, shed_sems.at[1])
    to_scalar = pltpu.make_async_copy(wanted_list, wanted_scalar, w_sems.at[3])
    to_scalar.start()
    to_scalar.wait()
    half = shed_out.shape[2] // 2
    for part in range(2):
        span = pl.ds(part * half, half)
        for i in range(shed_out.shape[0]):
            shed_out[i, :, span] = pages[wanted_scalar[0, i], :, span]
        send(
            shed_out.at[:, :, span], shed_in.at[:, :, span],
            shed_sems.at[2], shed_sems.at[3 + part], partner,
        )

    for load in inputs[2:]:
        load.wait()
    scaling = 1.0 / math.sqrt(HEAD)
    for g in range(GROUPS):
        for h in range(GROUP_HEADS):
            heads[g, h * ROWS : (h + 1) * ROWS, :] = queries[
                :, (g * GROUP_HEADS + h) * HEAD : (g * GROUP_HEADS + h + 1) * HEAD
            ]
    extra[...] = jnp.zeros_like(extra)
    extra[0:ROWS, :] = new_kv[...]
    table = page_table[...].astype(f32)
    diagonal = lax.broadcasted_iota(jnp.int32, (ROWS, ROWS), 0) == lax.broadcasted_iota(
        jnp.int32, (ROWS, ROWS), 1
    )
    length = jnp.sum(
        jnp.where(diagonal, lengths[...].astype(f32), 0.0), axis=1, keepdims=True
    )
    token = lax.broadcasted_iota(jnp.int32, (ROWS, TILE), 1)
    token_page = lax.div(token, PAGE).astype(f32)
    token_place = lax.rem(token, PAGE).astype(f32)

    def allowed(first_page):
        limit = jnp.zeros((ROWS, TILE), f32)
        for j in range(table.shape[1]):
            left = jnp.maximum(length - float(j * PAGE), 0.0)
            limit = limit + jnp.where(table[:, j : j + 1] == token_page + first_page, left, 0.0)
        return token_place < limit

    def masked(values, mask):
        width = values.shape[1]
        values = values.reshape(GROUP_HEADS, ROWS, width)
        return jnp.where(mask[None], values, masked_score).reshape(GROUP_HEADS * ROWS, width)

    def dot_last(left, right):
        return lax.dot_general(
            left, right, (((1,), (1,)), ((), ())), preferred_element_type=f32
        )

    new_mask = lax.broadcasted_iota(jnp.int32, (ROWS, EXTRA), 0) == lax.broadcasted_iota(
        jnp.int32, (ROWS, EXTRA), 1
    )
    for g in range(GROUPS):
        keys = extra[:, g * HEAD : (g + 1) * HEAD]
        values = masked(dot_last(heads[g], keys), new_mask)
        extra_scores[g] = values
        peak[g] = values
    tiles = own_pages // TILE_PAGES

    def score_tile(t, carry):
        mask = allowed((t * TILE_PAGES).astype(f32))
        for g in range(GROUPS):
            keys = pages[pl.ds(t * TILE_PAGES, TILE_PAGES), :, g * HEAD : (g + 1) * HEAD]
            values = masked(dot_last(heads[g], keys.reshape(TILE, HEAD)), mask)
            scores[g, t] = values
            peak[g] = jnp.maximum(peak[g], jnp.maximum(values[:, :128], values[:, 128:]))
        return carry

    lax.fori_loop(0, tiles, score_tile, 0)
    tops = []
    for g in range(GROUPS):
        top = jnp.max(peak[g], axis=1, keepdims=True)
        tops.append(top)
        weights = jnp.exp((extra_scores[g] - top) * scaling)
        weight_sum[g] = weights
        values = extra[:, (GROUPS + g) * HEAD : (GROUPS + g + 1) * HEAD]
        summed[g] = jnp.dot(weights.astype(bf16), values, preferred_element_type=f32)

    def weigh_tile(t, carry):
        for g in range(GROUPS):
            weights = jnp.exp((scores[g, t] - tops[g]) * scaling)
            weight_sum[g] += weights[:, :128] + weights[:, 128:]
            values = pages[
                pl.ds(t * TILE_PAGES, TILE_PAGES), :, (GROUPS + g) * HEAD : (GROUPS + g + 1) * HEAD
            ]
            summed[g] += jnp.dot(
                weights.astype(bf16), values.reshape(TILE, HEAD), preferred_element_type=f32
            )
        return carry

    lax.fori_loop(0, tiles, weigh_tile, 0)
    sums = [jnp.sum(weight_sum[g], axis=1, keepdims=True) for g in range(GROUPS)]

    settle(gathered, code_sems.at[1])

    row = lax.broadcasted_iota(jnp.int32, (256, 1), 0)
    lane = lax.broadcasted_iota(jnp.int32, (1, 128), 1)
    slot = lax.rem(row, 2)
    row_peer = lax.rem(lax.div(row, 2), PEERS)
    same_peer = row_peer == lax.div(lane, 16)
    lane_peer = lax.div(lax.broadcasted_iota(jnp.int32, (16, 128), 1), 16)
    for r, (a0, a1, a2) in enumerate(ROTATIONS):
        entries = jnp.where(lane_peer == 0, codes[...], 0.0)
        entries = jnp.where(lane_peer == SIDE, gathered[0], entries)
        for d in range(1, SIDE):
            for flip in (0, 1):
                entries = jnp.where(
                    lane_peer == flip * SIDE + d, gathered[a0 * 6 + d * 2 - 1 + flip], entries
                )
        where = list(place)
        where[a1] = lax.rem(place[a1] + lax.div(row, 64), SIDE)
        where[a2] = lax.rem(place[a2] + lax.rem(lax.div(row, 16), SIDE), SIDE)
        x, y, z = where
        expert = lax.div(z, 2) * 64 + x * 16 + lax.rem(z, 2) * 8 + y * 2 + core
        wanted = (expert * 2 + slot).astype(jnp.float32)
        chosen = jnp.zeros((256, 128), jnp.float32)
        gates = jnp.zeros((256, 128), jnp.float32)
        for k in range(8):
            match = same_peer & (entries[k : k + 1, :] == wanted)
            chosen = jnp.where(match, 1.0, chosen)
            gates = jnp.where(match, entries[8 + k : 9 + k, :], gates)
        select[r] = chosen.astype(jnp.bfloat16)
        gates = gates.T
        for part in range(3):
            piece = gates.astype(jnp.bfloat16)
            weight[r, part * 128 : (part + 1) * 128, :] = piece
            gates = gates - piece.astype(jnp.float32)


    shed_mask = allowed(float(own_pages))
    settle(shed_in.at[:, :, pl.ds(0, half)], shed_sems.at[3])
    late_parts = []
    for g in range(GROUPS):
        keys = shed_in[:, :, g * HEAD : (g + 1) * HEAD].reshape(TILE, HEAD)
        values = masked(dot_last(heads[g], keys), shed_mask)
        top = jnp.maximum(tops[g], jnp.max(values, axis=1, keepdims=True))
        again = jnp.exp((tops[g] - top) * scaling)
        weights = jnp.exp((values - top) * scaling)
        denominator = sums[g] * again + jnp.sum(weights, axis=1, keepdims=True)
        inverse = 1.0 / denominator
        summed[g] = summed[g] * (again * inverse)
        late_parts.append((weights.astype(bf16), inverse))
    settle(shed_in.at[:, :, pl.ds(half, half)], shed_sems.at[4])
    square = jnp.zeros((ROWS, HEAD), f32)
    for g in range(GROUPS):
        weights, inverse = late_parts[g]
        values = shed_in[:, :, (GROUPS + g) * HEAD : (GROUPS + g + 1) * HEAD].reshape(TILE, HEAD)
        total = summed[g] + jnp.dot(weights, values, preferred_element_type=f32) * inverse
        total = total.astype(bf16)
        for h in range(GROUP_HEADS):
            span = pl.ds((g * GROUP_HEADS + h) * HEAD, HEAD)
            part = total[h * ROWS : (h + 1) * ROWS, :]
            attended[:, span] = part
            joined = (residual[:, span].astype(f32) + part.astype(f32)).astype(bf16)
            merged[:, span] = joined
            joined = joined.astype(f32)
            square = square + joined * joined
    write_attended = pltpu.make_async_copy(attended, attended_out, w_sems.at[4])
    write_attended.start()
    width = queries.shape[1]
    mean = jnp.sum(square, axis=1, keepdims=True) * (1.0 / width)
    inverse = lax.rsqrt(mean + epsilon)
    normed[...] = (merged[...].astype(f32) * inverse * gain[...]).astype(bf16)

    sibling = other(0, 0, 1)
    send(normed, first.at[SIDE], core_sems.at[0], core_sems.at[1], sibling)
    for c, (r, start, count) in enumerate(CHUNKS):
        cols = columns(start, count)
        for d in (2, 1, 3):
            send(
                normed.at[:, cols], first.at[d, :, cols],
                sent.at[0], s1_r.at[c], other(ROTATIONS[r][0], d, 0),
            )
            if c < EARLY:
                send(
                    normed.at[:, cols], first.at[SIDE + d, :, cols],
                    core_sems.at[4], forward_r.at[c], other(ROTATIONS[r][0], d, 1),
                )
    first[0] = normed[...]

    def forward(c):
        cols = columns(*CHUNKS[c][1:])
        near = first.at[pl.ds(1, SIDE - 1), :, cols]
        settle(near, s1_r.at[c])
        if c < EARLY:
            return
        send(
            near, first.at[pl.ds(SIDE + 1, SIDE - 1), :, cols],
            core_sems.at[2], forward_r.at[c], sibling,
        )

    settle(first.at[SIDE], core_sems.at[1])
    for c, (r, start, count) in enumerate(CHUNKS):
        a1 = ROTATIONS[r][1]
        if c < EARLY:
            forward(c)
        if EARLY <= c + AHEAD < len(CHUNKS):
            forward(c + AHEAD)
        settle(first.at[pl.ds(SIDE + 1, SIDE - 1), :, columns(start, count)], forward_r.at[c])
        cols = columns(start, count)
        rows = first[:, :, cols].reshape(PEERS * 16, count * 128)
        block = jnp.dot(select[r], rows, preferred_element_type=jnp.float32).astype(jnp.bfloat16)
        block = block.reshape(SIDE, SIDE, 16, count * 128)
        for d in (2, 1, 3):
            packed[d, :, :, cols] = block[d]
        for d in (2, 1, 3):
            send(
                packed.at[d, :, :, cols], second.at[d, :, :, cols],
                sent.at[1], s2_r.at[c], other(a1, d, 0),
            )
        second[0, :, :, cols] = block[0]
    for c, (r, start, count) in enumerate(CHUNKS):
        a2 = ROTATIONS[r][2]
        settle(second.at[pl.ds(1, SIDE - 1), :, :, columns(start, count)], s2_r.at[c])
        cols = columns(start, count)
        for d in (2, 1, 3):
            send(
                second.at[:, d, :, cols], third.at[d, :, :, cols],
                sent.at[2], s3_r.at[c], other(a2, d, 0),
            )
        third[0, :, :, cols] = second[:, 0, :, cols]

    canon = lax.broadcasted_iota(jnp.int32, (256, 256), 0)
    local = lax.broadcasted_iota(jnp.int32, (256, 256), 1)
    apart = (
        lax.rem(lax.div(canon, 2), SIDE),
        lax.rem(lax.div(canon, 16), SIDE),
        lax.div(canon, 64),
    )
    flip = lax.rem(lax.div(canon, 8), 2) * 8
    orders = []
    for a0, a1, a2 in ROTATIONS:
        index = apart[a2] * 64 + apart[a1] * 16 + apart[a0] * 2 + lax.rem(canon, 2) + flip
        orders.append((index == local).astype(jnp.bfloat16))

    loads[0].wait()
    for c, (r, start, count) in enumerate(CHUNKS):
        cols = columns(start, count)
        settle(third.at[pl.ds(1, SIDE - 1), :, :, cols], s3_r.at[c])
        rows = third[:, :, :, cols].reshape(256, count * 128)
        if r:
            rows = jnp.dot(orders[r], rows, preferred_element_type=jnp.float32)
            rows = rows.astype(jnp.bfloat16)
        tokens[:, cols] = rows
        if r < 2:
            continue
        begin = CHUNKS[c - 2][1]
        span = columns(begin, start + count - begin)
        for n in range(0, 2 * hidden_dim, 512):
            piece = jnp.dot(
                tokens[:, span], gate_up[span, pl.ds(n, 512)],
                preferred_element_type=jnp.float32,
            )
            if c > 2:
                piece = product[:, pl.ds(n, 512)] + piece
            product[:, pl.ds(n, 512)] = piece
    gate = product[:, :hidden_dim]
    active = (gate / (1.0 + jnp.exp(-gate)) * product[:, hidden_dim:]).astype(jnp.bfloat16)
    hidden[0] = active

    loads[1].wait()
    for c, (r, start, count) in enumerate(CHUNKS):
        a2 = ROTATIONS[r][2]
        cols = columns(start, count)
        if c in (1, 2):
            turned = lax.dot_general(
                orders[r], active, (((0,), (0,)), ((), ())), preferred_element_type=jnp.float32
            )
            hidden[r] = turned.astype(jnp.bfloat16)
        finished = jnp.dot(hidden[r], down[:, cols], preferred_element_type=jnp.float32)
        finished = finished.astype(jnp.bfloat16).reshape(SIDE, SIDE, 16, count * 128)
        for d in (2, 1, 3):
            sent_back[d, :, :, cols] = finished[d]
        for d in (2, 1, 3):
            send(
                sent_back.at[d, :, :, cols], back_one.at[d, :, :, cols],
                sent.at[3], r3_r.at[c], other(a2, -d, 0),
            )
        back_one[0, :, :, cols] = finished[0]
    for c, (r, start, count) in enumerate(CHUNKS):
        a1 = ROTATIONS[r][1]
        settle(back_one.at[pl.ds(1, SIDE - 1), :, :, columns(start, count)], r3_r.at[c])
        cols = columns(start, count)
        for d in (2, 1, 3):
            send(
                back_one.at[:, d, :, cols], back_two.at[d, :, :, cols],
                sent.at[4], r2_r.at[c], other(a1, -d, 0),
            )
        back_two[0, :, :, cols] = back_one[:, 0, :, cols]
    def combine(c):
        r, start, count = CHUNKS[c]
        cols = columns(start, count)
        settle(back_two.at[pl.ds(1, SIDE - 1), :, :, cols], r2_r.at[c])
        results = back_two[:, :, :, cols].reshape(256, count * 128)
        parts = jnp.dot(weight[r], results, preferred_element_type=jnp.float32)
        total = parts[:128] + parts[128:256] + parts[256:]
        total = total.reshape(2, SIDE, 16, count * 128)
        if c >= LATE:
            expert_sum[:, cols] = total[0, 0]
            partial[0, :, :, cols] = total[1].astype(jnp.bfloat16)
            partial[1, 1:, :, cols] = total[0, 1:].astype(jnp.bfloat16)
            for d in (2, 1, 3):
                send(
                    partial.at[1, d, :, cols], back_three.at[d, :, cols],
                    sent.at[5], r1_r.at[c], other(ROTATIONS[r][0], -d, 0),
                )
                send(
                    partial.at[0, d, :, cols], from_core.at[d, :, cols],
                    core_sems.at[5], core_r.at[c], other(ROTATIONS[r][0], -d, 1),
                )
            send(
                partial.at[0, 0, :, cols], from_core.at[0, :, cols],
                core_sems.at[6], core_r.at[c], sibling,
            )
            return
        near_sum[:, :, cols] = total[0]
        partial[0, :, :, cols] = total[1].astype(jnp.bfloat16)
        send(
            partial.at[0, :, :, cols], from_core.at[:, :, cols],
            core_sems.at[3], core_r.at[c], sibling,
        )

    def pass_on(c):
        r, start, count = CHUNKS[c]
        cols = columns(start, count)
        settle(from_core.at[:, :, cols], core_r.at[c])
        total = near_sum[:, :, cols] + from_core[:, :, cols].astype(jnp.float32)
        expert_sum[:, cols] = total[0]
        partial[1, 1:, :, cols] = total[1:].astype(jnp.bfloat16)
        for d in (2, 1, 3):
            send(
                partial.at[1, d, :, cols], back_three.at[d, :, cols],
                sent.at[5], r1_r.at[c], other(ROTATIONS[r][0], -d, 0),
            )

    for step in range(len(CHUNKS)):
        combine(step)
        if 0 <= step - BEHIND < LATE:
            pass_on(step - BEHIND)
    for c, (r, start, count) in enumerate(CHUNKS):
        cols = columns(start, count)
        settle(back_three.at[pl.ds(1, SIDE - 1), :, cols], r1_r.at[c])
        total = expert_sum[:, cols]
        for d in range(1, SIDE):
            total = total + back_three[d, :, cols].astype(jnp.float32)
        if c >= LATE:
            settle(from_core.at[:, :, cols], core_r.at[c])
            for d in range(SIDE):
                total = total + from_core[d, :, cols].astype(jnp.float32)
        merged[:, cols] = (merged[:, cols].astype(jnp.float32) + total).astype(jnp.bfloat16)
        pltpu.make_async_copy(merged.at[:, cols], layer_out.at[:, cols], w_sems.at[5]).start()
    settle(shed_list, shed_sems.at[0])
    settle(gathered, code_sems.at[0])
    settle(shed_out, shed_sems.at[2])
    settle(normed, core_sems.at[0])
    width = normed.shape[1]
    early = CHUNKS[EARLY][1] * 128
    late = CHUNKS[LATE][1] * 128
    far = pl.ds(SIDE + 1, SIDE - 1)
    settle(first.at[far, :, pl.ds(early, width - early)], core_sems.at[2])
    settle(first.at[far, :, pl.ds(0, early)], core_sems.at[4])
    settle(from_core.at[:, :, pl.ds(0, late)], core_sems.at[3])
    settle(from_core.at[pl.ds(1, SIDE - 1), :, pl.ds(late, width - late)], core_sems.at[5])
    settle(from_core.at[0, :, pl.ds(late, width - late)], core_sems.at[6])
    for i, region in enumerate(
        (
            first.at[pl.ds(1, SIDE - 1)], packed.at[pl.ds(1, SIDE - 1)],
            third.at[pl.ds(1, SIDE - 1)], sent_back.at[pl.ds(1, SIDE - 1)],
            back_two.at[pl.ds(1, SIDE - 1)], partial.at[1, pl.ds(1, SIDE - 1)],
        )
    ):
        settle(region, sent.at[i])
    write_attended.wait()
    settle(merged, w_sems.at[5])


def local(
    queries, new_kv, kv_pages, page_table, lengths, shed_slots, residual, norm_gain,
    expert_ids, gate_weights, w_gate_up, w_down,
):
    rows, width = queries.shape
    gate_up, down = w_gate_up[0], w_down[0]
    hidden_dim = down.shape[0]
    pages, page, kv_width = kv_pages.shape
    shed = shed_slots.shape[0]
    chunks = len(CHUNKS)
    bf16, f32 = jnp.bfloat16, jnp.float32
    hbm = pl.BlockSpec(memory_space=pl.ANY)
    block = pltpu.VMEM((SIDE, SIDE, 16, width), bf16)
    peers = pltpu.VMEM((PEERS, 16, width), bf16)
    dma = pltpu.SemaphoreType.DMA
    group_rows = GROUP_HEADS * ROWS
    attended, layer_out = pl.pallas_call(
        layer_kernel,
        out_shape=(
            jax.ShapeDtypeStruct((rows, width), bf16),
            jax.ShapeDtypeStruct((rows, width), bf16),
        ),
        in_specs=[hbm] * 12,
        out_specs=(hbm, hbm),
        scratch_shapes=[
            pltpu.VMEM((rows, width), bf16),
            pltpu.VMEM((rows, kv_width), bf16),
            pltpu.VMEM(page_table.shape, jnp.int32),
            pltpu.VMEM((1, rows), jnp.int32),
            pltpu.VMEM((rows, width), bf16),
            pltpu.VMEM((1, width), f32),
            pltpu.VMEM((8, rows), jnp.int32),
            pltpu.VMEM((8, rows), f32),
            pltpu.VMEM((rows, width), bf16),
            pltpu.VMEM((rows, width), bf16),
            pltpu.VMEM((rows, width), f32),
            pltpu.VMEM((pages, page, kv_width), bf16),
            pltpu.VMEM((EXTRA, kv_width), bf16),
            pltpu.VMEM((1, shed), jnp.int32),
            pltpu.SMEM((1, shed), jnp.int32),
            pltpu.VMEM((shed, page, kv_width), bf16),
            pltpu.VMEM((shed, page, kv_width), bf16),
            pltpu.VMEM((GROUPS, group_rows, HEAD), bf16),
            pltpu.VMEM((GROUPS, pages // TILE_PAGES, group_rows, TILE), f32),
            pltpu.VMEM((GROUPS, group_rows, EXTRA), f32),
            pltpu.VMEM((GROUPS, group_rows, 128), f32),
            pltpu.VMEM((GROUPS, group_rows, 128), f32),
            pltpu.VMEM((GROUPS, group_rows, HEAD), f32),
            pltpu.VMEM((rows, width), bf16),
            pltpu.VMEM((16, 128), f32),
            pltpu.VMEM(gate_up.shape, bf16),
            pltpu.VMEM(down.shape, bf16),
            pltpu.VMEM((19, 16, 128), f32),
            pltpu.VMEM((3, 256, 128), bf16),
            pltpu.VMEM((3, 3 * 128, 256), bf16),
            peers,
            block,
            block,
            block,
            pltpu.VMEM((256, width), bf16),
            pltpu.VMEM((256, 2 * hidden_dim), f32),
            pltpu.VMEM((3, 256, hidden_dim), bf16),
            block,
            block,
            block,
            pltpu.VMEM((2, SIDE, 16, width), bf16),
            pltpu.VMEM((SIDE, 16, width), f32),
            pltpu.VMEM((SIDE, 16, width), bf16),
            pltpu.VMEM((SIDE, 16, width), bf16),
            dma((6,)), dma((8,)), dma((5,)), dma((2,)), dma((6,)), dma((7,)),
            dma((chunks,)), dma((chunks,)), dma((chunks,)),
            dma((chunks,)), dma((chunks,)), dma((chunks,)),
            dma((chunks,)), dma((chunks,)),
        ],
        compiler_params=pltpu.CompilerParams(
            collective_id=0, has_side_effects=True, vmem_limit_bytes=52 * 1024 * 1024
        ),
    )(
        *(
            pltpu.with_memory_space_constraint(value, pltpu.HBM)
            for value in (
                queries, new_kv, kv_pages, page_table, lengths.reshape(1, rows),
                shed_slots.reshape(1, shed), residual, norm_gain.reshape(1, width),
                expert_ids.T, gate_weights.T, gate_up, down,
            )
        )
    )
    return (attended, layer_out)


def solution(mesh):
    return jax.shard_map(
        local,
        mesh=mesh,
        in_specs=(
            P(("pool", "dev"), None),
            P(("pool", "dev"), None),
            P(("pool", "dev"), None, None),
            P(("pool", "dev"), None),
            P(("pool", "dev")),
            P(("pool", "dev")),
            P(("pool", "dev"), None),
            P(),
            P(("pool", "dev"), None),
            P(("pool", "dev"), None),
            P(("pool", "dev"), None, None),
            P(("pool", "dev"), None, None),
        ),
        out_specs=(P(("pool", "dev"), None), P(("pool", "dev"), None)),
        check_vma=False,
    )
```
